512 devices in a mesh: rows: 64 (over y, z_hi, core), rep: 8 (over x, z_lo).
Axes of the slice: x: 4, y: 8, z: 8 (z_hi: 4, z_lo: 2; z = z_hi * 2 + z_lo), core: 2. Of those that a mesh axis runs over, the one named last changes fastest.
Arguments:
- features: bfloat16 [32768, 128], P('rows'), may hold values from -6 to 6
- degree: int32 [32768], P('rows'), may hold values from 32 to 320
- tile_block: int32 [256, 64, 8], P('rows', 'rep'), may hold values from 0 to 3
- edge_count: int32 [256, 64, 8], P('rows', 'rep'), may hold values from 0 to 128, as said below
- edge_code: int32 [256, 64, 8, 128], P('rows', 'rep'), may hold values from 0 to 16368
- weight: bfloat16 [128, 256], replicated, may hold values from -3 to 3
- bias: float32 [256], replicated, may hold values from -3 to 3
- cotangent: bfloat16 [32768, 256], P(('rows', 'rep')), may hold values from -0.03125 to 0.03125
Outputs:
- activated: bfloat16 [32768, 256], P(('rows', 'rep'))
- grad_weight: float32 [128, 256], replicated
- grad_bias: float32 [256], replicated
The draws below stay inside these ranges and needn't reach their ends.
Inputs may be any that keep to these rules, and one draw needn't show every extreme that they name: Only the first edge_count entries of a tile's edge codes are live; some tiles hold 128 live edges.
All inputs are finite; a program needn't handle non-finite values.
Results may differ from the reference program's by a relative error of at most 0.0063.
Values may be sent and summed in bfloat16 or wider, within the bound.
No kernel may reach another device: no remote copies, remote signals or barrier semaphores. Data moves between devices by JAX's collectives and lax.ppermute only.
A program may use at most 64 MiB of HBM per device.

```python
import jax
import jax.numpy as jnp
from jax import lax

F = 128
H = 256
BLK_DEV = 4
KQ = 8
ECAP = 128
GROUPS = 64
BLOCKS = 256
NODES = 32768
N_ROWS = 64


def draw_edge_count(key, part):
    key_scale, key_base, key_full = jax.random.split(key, 3)
    load_scale = jax.random.randint(key_scale, (BLOCKS, 1, 1), 1, 5)
    counts_base = jax.random.randint(key_base, (BLOCKS, GROUPS, KQ), 0, ECAP // 4 + 1) * load_scale
    is_full = jax.random.randint(key_full, (BLOCKS, GROUPS, KQ), 0, 16) == 0
    return jnp.where(is_full, ECAP, jnp.minimum(counts_base, ECAP)).astype(jnp.int32)


def touch_ends(values, own_key, least, top_value):
    dims = values.shape
    index_at = [jax.random.randint(jax.random.fold_in(own_key, axis), (), 0, dims[axis]) for axis in range(len(dims))]
    values = values.at[tuple(index_at)].set(least)
    longest = dims.index(max(dims))
    index_at[longest] = (index_at[longest] + 1) % dims[longest]
    return values.at[tuple(index_at)].set(top_value)


def block_levels(rng, extent, cuts, low, top_value):
    level = 1.0
    for position, shards_of in cuts:
        heights = jax.random.uniform(jax.random.fold_in(jax.random.fold_in(rng, 6), position), (shards_of,), jnp.float32, low / len(cuts), top_value / len(cuts))
        level = level * jnp.repeat(jnp.exp(heights), extent[position] // shards_of).reshape((-1,) + (1,) * (len(extent) - 1 - position))
    return level


def bell_draw(key, extent, scale, limit, cuts=(), held_as=jnp.bfloat16):
    loudness = block_levels(key, extent, cuts, -0.22, 0.18) if cuts else 1.0
    array = jax.random.normal(key, extent, jnp.float32) * scale * loudness
    return jnp.minimum(jnp.maximum(array, -limit), limit).astype(held_as)


def setup_inputs(seed: int = 0) -> dict:
    key_of = jax.random.split(jax.random.key(seed), 9)
    features = bell_draw(key_of[0], (NODES, F), 1.0, 6.0, ((0, 64),))
    degree = touch_ends(jax.random.randint(key_of[1], (NODES,), 32, 321), jax.random.fold_in(key_of[1], 1), 32, 320).astype(jnp.int32)
    tile_block = touch_ends(jax.random.randint(key_of[2], (BLOCKS, GROUPS, KQ), 0, BLK_DEV), jax.random.fold_in(key_of[2], 1), 0, BLK_DEV - 1).astype(jnp.int32)
    edge_count = draw_edge_count(jax.random.fold_in(key_of[8], 71), 0)
    edge_code = touch_ends(jax.random.randint(key_of[4], (BLOCKS, GROUPS, KQ, ECAP), 0, 16369), jax.random.fold_in(key_of[4], 1), 0, 16368).astype(jnp.int32)
    weight = bell_draw(key_of[5], (F, H), (F // 32) ** -0.5, 3.0)
    bias = bell_draw(key_of[6], (H,), 0.5, 3.0, (), jnp.float32)
    cotangent = bell_draw(key_of[7], (NODES, H), (NODES ** -0.5), 0.03125, ((0, 512),))
    return dict(features=features, degree=degree, tile_block=tile_block, edge_count=edge_count, edge_code=edge_code, weight=weight, bias=bias, cotangent=cotangent)


def gelu_tanh(values):
    return jax.nn.gelu(values, approximate=True)

def reference(features, degree, tile_block, edge_count, edge_code, weight, bias, cotangent):
    inv_deg = lax.rsqrt(degree.astype(jnp.float32))
    scaled = (features.astype(jnp.float32) * inv_deg[:, None]).astype(jnp.bfloat16)
    scaled_table = scaled.astype(jnp.float32)
    offsets = jnp.arange(N_ROWS, dtype=jnp.int32)
    slot_iota = jnp.arange(ECAP, dtype=jnp.int32)

    def one_block(inputs):
        block_index, block_ids, live_count, codes = inputs
        group_id = block_index // BLK_DEV
        owner_group = (group_id + offsets) % N_ROWS
        column_block = owner_group[:, None] * BLK_DEV + block_ids
        far_node = column_block[:, :, None] * 128 + codes % 128
        is_live = slot_iota[None, None, :] < live_count[:, :, None]
        values = jnp.where(is_live[..., None], scaled_table[far_node], 0.0)
        return jax.ops.segment_sum(values.reshape(-1, F), (codes // 128).reshape(-1), num_segments=128)
    edge_sums = lax.map(one_block, (jnp.arange(BLOCKS, dtype=jnp.int32), tile_block, edge_count, edge_code))
    edge_sums = edge_sums.reshape(NODES, F)
    aggregate = (inv_deg[:, None] * (edge_sums + scaled_table)).astype(jnp.bfloat16)
    pre_act = jnp.dot(aggregate, weight, preferred_element_type=jnp.float32) + bias
    activated, pull_back = jax.vjp(gelu_tanh, pre_act)
    delta = pull_back(cotangent.astype(jnp.float32))[0].astype(jnp.bfloat16)
    grad_weight = jnp.dot(aggregate.T, delta, preferred_element_type=jnp.float32)
    grad_bias = lax.optimization_barrier(jnp.sum(delta.astype(jnp.float32), axis=0))
    return (activated.astype(jnp.bfloat16), grad_weight, grad_bias)
```

```python
import jax
import jax.numpy as jnp
from jax import lax
from jax.sharding import PartitionSpec as P

BFLY_BITS = (3, 0, 1, 6, 4, 2, 7, 5, 8)


def from_behind(value, axis, steps):
    count = lax.axis_size(axis)
    pairs = [(source, (source + steps) % count) for source in range(count)]
    return lax.ppermute(value, axis, pairs)


def butterfly_sum(value, axes, count):
    for bit in BFLY_BITS:
        if (1 << bit) >= count:
            continue
        pairs = [(source, source ^ (1 << bit)) for source in range(count)]
        value = value + lax.ppermute(value, axes, pairs)
    return value


def halving_scatter(value, axis):
    count = lax.axis_size(axis)
    me = lax.axis_index(axis)
    levels = count.bit_length() - 1
    share = value.shape[0] // count
    buf = value.reshape((2,) * levels + (share,) + value.shape[1:])
    for bit in range(levels):
        dim = levels - 1 - bit
        mine = (me >> bit) & 1
        keep = lax.dynamic_index_in_dim(buf, mine, dim, keepdims=False)
        send = lax.dynamic_index_in_dim(buf, 1 - mine, dim, keepdims=False)
        pairs = [(source, source ^ (1 << bit)) for source in range(count)]
        buf = keep + lax.ppermute(send, axis, pairs)
    return buf


def gelu_tanh(values):
    return jax.nn.gelu(values, approximate=True)


def tile_sums(buffer, offset, tile_block, edge_count, edge_code):
    block_ids = lax.dynamic_index_in_dim(tile_block, offset, 1, keepdims=False)
    live_count = lax.dynamic_index_in_dim(edge_count, offset, 1, keepdims=False)
    codes = lax.dynamic_index_in_dim(edge_code, offset, 1, keepdims=False)
    block_total, slot_count, edge_cap = codes.shape
    feat_width = buffer.shape[1]
    far_node = block_ids[:, :, None] * 128 + codes % 128
    picked = jnp.take(buffer, far_node.reshape(-1), axis=0).reshape(
        block_total, slot_count, edge_cap, feat_width
    )
    is_live = lax.broadcasted_iota(jnp.int32, codes.shape, 2) < live_count[:, :, None]
    target = jnp.where(is_live, codes // 128, -1)
    row_iota = lax.broadcasted_iota(jnp.int32, (1, 1, 128, 1), 2)
    onehot = (target[:, :, None, :] == row_iota).astype(jnp.bfloat16)
    summed = jnp.einsum("bkre,bkef->brf", onehot, picked, preferred_element_type=jnp.float32)
    return summed.reshape(block_total * 128, feat_width)


def local(features, degree, tile_block, edge_count, edge_code, weight, bias, cotangent):
    step_count = tile_block.shape[1]
    replicas = lax.axis_size("rep")
    replica = lax.axis_index("rep")
    devices = lax.axis_size("rows") * replicas
    inv_deg = lax.rsqrt(degree.astype(jnp.float32))
    scaled = (features.astype(jnp.float32) * inv_deg[:, None]).astype(jnp.bfloat16)

    def local_sums(buffer, offset):
        return tile_sums(buffer, offset, tile_block, edge_count, edge_code)

    buffer = scaled
    for bit_index in range(replicas.bit_length() - 1):
        shifted = from_behind(buffer, "rows", -(step_count << bit_index))
        select = replica // (1 << bit_index) % 2 == 1
        buffer = jnp.where(select, shifted, buffer)
    partial_total = local_sums(buffer, 0)

    def advance(step_index, loop_state):
        current, running = loop_state
        current = from_behind(current, "rows", -1)
        return (current, running + local_sums(current, step_index))

    buffer, partial_total = lax.fori_loop(1, step_count, advance, (buffer, partial_total))
    edge_sums = halving_scatter(partial_total, "rep")
    share_rows = edge_sums.shape[0]
    share_start = replica * share_rows
    own_rows = lax.dynamic_slice_in_dim(scaled, share_start, share_rows, 0).astype(jnp.float32)
    own_inv = lax.dynamic_slice_in_dim(inv_deg, share_start, share_rows, 0)
    aggregate = (own_inv[:, None] * (edge_sums + own_rows)).astype(jnp.bfloat16)
    pre_act = jnp.dot(aggregate, weight, preferred_element_type=jnp.float32) + bias
    activated, pull_back = jax.vjp(gelu_tanh, pre_act)
    delta_bf = pull_back(cotangent.astype(jnp.float32))[0].astype(jnp.bfloat16)
    local_weight = lax.dot_general(
        aggregate, delta_bf, (((0,), (0,)), ((), ())), preferred_element_type=jnp.float32
    )
    local_bias = jnp.sum(delta_bf.astype(jnp.float32), axis=0)
    feat_rows = local_weight.shape[0]
    packed = jnp.concatenate(
        [local_weight, jnp.broadcast_to(local_bias[None, :], (8, local_bias.shape[0]))], axis=0
    )
    packed = butterfly_sum(packed, ("rows", "rep"), devices)
    grad_weight = packed[:feat_rows]
    grad_bias = packed[feat_rows]
    return (activated.astype(jnp.bfloat16), grad_weight, grad_bias)


def solution(mesh):
    in_specs = (
        P("rows", None),
        P("rows"),
        P("rows", "rep", None),
        P("rows", "rep", None),
        P("rows", "rep", None, None),
        P(),
        P(),
        P(("rows", "rep"), None),
    )
    out_specs = (P(("rows", "rep"), None), P(), P())
    return jax.shard_map(local, mesh=mesh, in_specs=in_specs, out_specs=out_specs, check_vma=False)
```

```python
import jax
import jax.numpy as jnp
from jax import lax
from jax.sharding import PartitionSpec as P

BFLY_BITS = (3, 0, 1, 6, 4, 2, 7, 5, 8)


def from_behind(value, axis, steps):
    count = lax.axis_size(axis)
    pairs = [(source, (source + steps) % count) for source in range(count)]
    return lax.ppermute(value, axis, pairs)


def butterfly_sum(value, axes, count):
    for bit in BFLY_BITS:
        if (1 << bit) >= count:
            continue
        pairs = [(source, source ^ (1 << bit)) for source in range(count)]
        value = value + lax.ppermute(value, axes, pairs)
    return value


def halving_scatter(value, axis):
    count = lax.axis_size(axis)
    me = lax.axis_index(axis)
    levels = count.bit_length() - 1
    share = value.shape[0] // count
    buf = value.reshape((2,) * levels + (share,) + value.shape[1:])
    for bit in range(levels):
        dim = levels - 1 - bit
        mine = (me >> bit) & 1
        keep = lax.dynamic_index_in_dim(buf, mine, dim, keepdims=False)
        send = lax.dynamic_index_in_dim(buf, 1 - mine, dim, keepdims=False)
        pairs = [(source, source ^ (1 << bit)) for source in range(count)]
        buf = keep + lax.ppermute(send, axis, pairs)
    return buf


def gelu_tanh(values):
    return jax.nn.gelu(values, approximate=True)


def tile_sums(buffer, offset, tile_block, edge_count, edge_code):
    block_ids = lax.dynamic_index_in_dim(tile_block, offset, 1, keepdims=False)
    live_count = lax.dynamic_index_in_dim(edge_count, offset, 1, keepdims=False)
    codes = lax.dynamic_index_in_dim(edge_code, offset, 1, keepdims=False)
    block_total, slot_count, edge_cap = codes.shape
    feat_width = buffer.shape[1]
    far_node = block_ids[:, :, None] * 128 + codes % 128
    col_iota = lax.broadcasted_iota(jnp.int32, (1, 1, 1, buffer.shape[0]), 3)
    onehot_col = (far_node[..., None] == col_iota).astype(jnp.bfloat16)
    picked = jnp.einsum(
        "bkec,cf->bkef", onehot_col, buffer, preferred_element_type=jnp.float32
    ).astype(jnp.bfloat16)
    is_live = lax.broadcasted_iota(jnp.int32, codes.shape, 2) < live_count[:, :, None]
    target = jnp.where(is_live, codes // 128, -1)
    row_iota = lax.broadcasted_iota(jnp.int32, (1, 1, 128, 1), 2)
    onehot = (target[:, :, None, :] == row_iota).astype(jnp.bfloat16)
    summed = jnp.einsum("bkre,bkef->brf", onehot, picked, preferred_element_type=jnp.float32)
    return summed.reshape(block_total * 128, feat_width)


def local(features, degree, tile_block, edge_count, edge_code, weight, bias, cotangent):
    step_count = tile_block.shape[1]
    replicas = lax.axis_size("rep")
    replica = lax.axis_index("rep")
    devices = lax.axis_size("rows") * replicas
    inv_deg = lax.rsqrt(degree.astype(jnp.float32))
    scaled = (features.astype(jnp.float32) * inv_deg[:, None]).astype(jnp.bfloat16)

    def local_sums(buffer, offset):
        return tile_sums(buffer, offset, tile_block, edge_count, edge_code)

    row_count = lax.axis_size("rows")
    pairs = []
    for rep_index in range(replicas):
        for source in range(row_count):
            target = (source - step_count * rep_index) % row_count
            pairs.append((source * replicas + rep_index, target * replicas + rep_index))
    current = lax.ppermute(scaled, ("rows", "rep"), pairs)
    partial_total = None
    for step_index in range(step_count):
        if step_index + 1 < step_count:
            following = from_behind(current, "rows", -1)
        sums = local_sums(current, step_index)
        partial_total = sums if partial_total is None else partial_total + sums
        if step_index + 1 < step_count:
            current = following
    edge_sums = halving_scatter(partial_total, "rep")
    share_rows = edge_sums.shape[0]
    share_start = replica * share_rows
    own_rows = lax.dynamic_slice_in_dim(scaled, share_start, share_rows, 0).astype(jnp.float32)
    own_inv = lax.dynamic_slice_in_dim(inv_deg, share_start, share_rows, 0)
    aggregate = (own_inv[:, None] * (edge_sums + own_rows)).astype(jnp.bfloat16)
    pre_act = jnp.dot(aggregate, weight, preferred_element_type=jnp.float32) + bias
    activated, pull_back = jax.vjp(gelu_tanh, pre_act)
    delta_bf = pull_back(cotangent.astype(jnp.float32))[0].astype(jnp.bfloat16)
    local_weight = lax.dot_general(
        aggregate, delta_bf, (((0,), (0,)), ((), ())), preferred_element_type=jnp.float32
    )
    local_bias = jnp.sum(delta_bf.astype(jnp.float32), axis=0)
    feat_rows = local_weight.shape[0]
    packed = jnp.concatenate(
        [local_weight, jnp.broadcast_to(local_bias[None, :], (8, local_bias.shape[0]))], axis=0
    )
    packed = butterfly_sum(packed, ("rows", "rep"), devices)
    grad_weight = packed[:feat_rows]
    grad_bias = packed[feat_rows]
    return (activated.astype(jnp.bfloat16), grad_weight, grad_bias)


def solution(mesh):
    in_specs = (
        P("rows", None),
        P("rows"),
        P("rows", "rep", None),
        P("rows", "rep", None),
        P("rows", "rep", None, None),
        P(),
        P(),
        P(("rows", "rep"), None),
    )
    out_specs = (P(("rows", "rep"), None), P(), P())
    return jax.shard_map(local, mesh=mesh, in_specs=in_specs, out_specs=out_specs, check_vma=False)
```

```python
import jax
import jax.numpy as jnp
from jax import lax
from jax.sharding import PartitionSpec as P

ROWS_BITS = (0, 3, 1, 4, 2, 5)
REP_BITS = (0, 1, 2)


def from_behind(value, axis, steps):
    count = lax.axis_size(axis)
    pairs = [(source, (source + steps) % count) for source in range(count)]
    return lax.ppermute(value, axis, pairs)


def butterfly_sum(value, axis, order):
    count = lax.axis_size(axis)
    for bit in order:
        if (1 << bit) >= count:
            continue
        pairs = [(source, source ^ (1 << bit)) for source in range(count)]
        value = value + lax.ppermute(value, axis, pairs)
    return value


def halving_scatter(value, axis):
    count = lax.axis_size(axis)
    me = lax.axis_index(axis)
    levels = count.bit_length() - 1
    share = value.shape[0] // count
    buf = value.reshape((2,) * levels + (share,) + value.shape[1:])
    for bit in range(levels):
        dim = levels - 1 - bit
        mine = (me >> bit) & 1
        keep = lax.dynamic_index_in_dim(buf, mine, dim, keepdims=False)
        send = lax.dynamic_index_in_dim(buf, 1 - mine, dim, keepdims=False)
        pairs = [(source, source ^ (1 << bit)) for source in range(count)]
        buf = keep + lax.ppermute(send, axis, pairs)
    return buf


def gelu_tanh(values):
    return jax.nn.gelu(values, approximate=True)


def tile_sums(buffer, offset, tile_block, edge_count, edge_code):
    block_ids = lax.dynamic_index_in_dim(tile_block, offset, 1, keepdims=False)
    live_count = lax.dynamic_index_in_dim(edge_count, offset, 1, keepdims=False)
    codes = lax.dynamic_index_in_dim(edge_code, offset, 1, keepdims=False)
    block_total, slot_count, edge_cap = codes.shape
    feat_width = buffer.shape[1]
    far_node = block_ids[:, :, None] * 128 + codes % 128
    col_iota = lax.broadcasted_iota(jnp.int32, (1, 1, 1, buffer.shape[0]), 3)
    onehot_col = (far_node[..., None] == col_iota).astype(jnp.bfloat16)
    picked = jnp.einsum(
        "bkec,cf->bkef", onehot_col, buffer, preferred_element_type=jnp.float32
    ).astype(jnp.bfloat16)
    is_live = lax.broadcasted_iota(jnp.int32, codes.shape, 2) < live_count[:, :, None]
    target = jnp.where(is_live, codes // 128, -1)
    row_iota = lax.broadcasted_iota(jnp.int32, (1, 1, 128, 1), 2)
    onehot = (target[:, :, None, :] == row_iota).astype(jnp.bfloat16)
    summed = jnp.einsum("bkre,bkef->brf", onehot, picked, preferred_element_type=jnp.float32)
    return summed.reshape(block_total * 128, feat_width)


def local(features, degree, tile_block, edge_count, edge_code, weight, bias, cotangent):
    step_count = tile_block.shape[1]
    replicas = lax.axis_size("rep")
    replica = lax.axis_index("rep")
    inv_deg = lax.rsqrt(degree.astype(jnp.float32))
    scaled = (features.astype(jnp.float32) * inv_deg[:, None]).astype(jnp.bfloat16)

    def local_sums(buffer, offset):
        return tile_sums(buffer, offset, tile_block, edge_count, edge_code)

    row_count = lax.axis_size("rows")
    pairs = []
    for rep_index in range(replicas):
        for source in range(row_count):
            target = (source - step_count * rep_index) % row_count
            pairs.append((source * replicas + rep_index, target * replicas + rep_index))
    held = lax.ppermute(scaled, ("rows", "rep"), pairs)[None]
    cot_group = lax.all_gather(cotangent, "rep", axis=0, tiled=True)
    partial_total = local_sums(held[0], 0)
    while held.shape[0] < step_count:
        have = held.shape[0]
        arrived = from_behind(held, "rows", -have)
        for extra in range(arrived.shape[0]):
            partial_total = partial_total + local_sums(arrived[extra], have + extra)
        held = jnp.concatenate([held, arrived], axis=0)
    edge_sums = butterfly_sum(partial_total, "rep", REP_BITS)
    aggregate = (inv_deg[:, None] * (edge_sums + scaled.astype(jnp.float32))).astype(jnp.bfloat16)
    pre_act = jnp.dot(aggregate, weight, preferred_element_type=jnp.float32) + bias
    activated, pull_back = jax.vjp(gelu_tanh, pre_act)
    delta_bf = pull_back(cot_group.astype(jnp.float32))[0].astype(jnp.bfloat16)
    local_weight = lax.dot_general(
        aggregate, delta_bf, (((0,), (0,)), ((), ())), preferred_element_type=jnp.float32
    )
    local_bias = jnp.sum(delta_bf.astype(jnp.float32), axis=0)
    feat_rows = local_weight.shape[0]
    packed = jnp.concatenate(
        [local_weight, jnp.broadcast_to(local_bias[None, :], (8, local_bias.shape[0]))], axis=0
    )
    packed = butterfly_sum(packed, "rows", ROWS_BITS)
    grad_weight = packed[:feat_rows]
    grad_bias = packed[feat_rows]
    share_rows = cotangent.shape[0]
    own_act = lax.dynamic_slice_in_dim(activated, replica * share_rows, share_rows, 0)
    return (own_act.astype(jnp.bfloat16), grad_weight, grad_bias)


def solution(mesh):
    in_specs = (
        P("rows", None),
        P("rows"),
        P("rows", "rep", None),
        P("rows", "rep", None),
        P("rows", "rep", None, None),
        P(),
        P(),
        P(("rows", "rep"), None),
    )
    out_specs = (P(("rows", "rep"), None), P(), P())
    return jax.shard_map(local, mesh=mesh, in_specs=in_specs, out_specs=out_specs, check_vma=False)
```

```python
import jax
import jax.numpy as jnp
from jax import lax
from jax.sharding import PartitionSpec as P

ROWS_BITS = (0, 3, 1, 4, 2, 5)
REP_BITS = (0, 1, 2)


def from_behind(value, axis, steps):
    count = lax.axis_size(axis)
    pairs = [(source, (source + steps) % count) for source in range(count)]
    return lax.ppermute(value, axis, pairs)


def butterfly_sum(value, axis, order):
    count = lax.axis_size(axis)
    for bit in order:
        if (1 << bit) >= count:
            continue
        pairs = [(source, source ^ (1 << bit)) for source in range(count)]
        value = value + lax.ppermute(value, axis, pairs)
    return value


def halving_scatter(value, axis):
    count = lax.axis_size(axis)
    me = lax.axis_index(axis)
    levels = count.bit_length() - 1
    share = value.shape[0] // count
    buf = value.reshape((2,) * levels + (share,) + value.shape[1:])
    for bit in range(levels):
        dim = levels - 1 - bit
        mine = (me >> bit) & 1
        keep = lax.dynamic_index_in_dim(buf, mine, dim, keepdims=False)
        send = lax.dynamic_index_in_dim(buf, 1 - mine, dim, keepdims=False)
        pairs = [(source, source ^ (1 << bit)) for source in range(count)]
        buf = keep + lax.ppermute(send, axis, pairs)
    return buf


def gelu_tanh(values):
    return jax.nn.gelu(values, approximate=True)


def tile_sums(buffer, offset, tile_block, edge_count, edge_code):
    block_ids = lax.dynamic_index_in_dim(tile_block, offset, 1, keepdims=False)
    live_count = lax.dynamic_index_in_dim(edge_count, offset, 1, keepdims=False)
    codes = lax.dynamic_index_in_dim(edge_code, offset, 1, keepdims=False)
    block_total, slot_count, edge_cap = codes.shape
    feat_width = buffer.shape[1]
    far_node = block_ids[:, :, None] * 128 + codes % 128
    col_iota = lax.broadcasted_iota(jnp.int32, (1, 1, 1, buffer.shape[0]), 3)
    onehot_col = (far_node[..., None] == col_iota).astype(jnp.bfloat16)
    picked = jnp.einsum(
        "bkec,cf->bkef", onehot_col, buffer, preferred_element_type=jnp.float32
    ).astype(jnp.bfloat16)
    is_live = lax.broadcasted_iota(jnp.int32, codes.shape, 2) < live_count[:, :, None]
    target = jnp.where(is_live, codes // 128, -1)
    row_iota = lax.broadcasted_iota(jnp.int32, (1, 1, 128, 1), 2)
    onehot = (target[:, :, None, :] == row_iota).astype(jnp.bfloat16)
    summed = jnp.einsum("bkre,bkef->brf", onehot, picked, preferred_element_type=jnp.float32)
    return summed.reshape(block_total * 128, feat_width)


def local(features, degree, tile_block, edge_count, edge_code, weight, bias, cotangent):
    step_count = tile_block.shape[1]
    replicas = lax.axis_size("rep")
    replica = lax.axis_index("rep")
    inv_deg = lax.rsqrt(degree.astype(jnp.float32))
    scaled = (features.astype(jnp.float32) * inv_deg[:, None]).astype(jnp.bfloat16)

    def local_sums(buffer, offset):
        return tile_sums(buffer, offset, tile_block, edge_count, edge_code)

    row_count = lax.axis_size("rows")
    pairs = []
    for rep_index in range(replicas):
        for source in range(row_count):
            target = (source - step_count * rep_index) % row_count
            pairs.append((source * replicas + rep_index, target * replicas + rep_index))
    held = lax.ppermute(scaled, ("rows", "rep"), pairs)[None]
    partial_total = local_sums(held[0], 0)
    while held.shape[0] < step_count:
        have = held.shape[0]
        arrived = from_behind(held, "rows", -have)
        for extra in range(arrived.shape[0]):
            partial_total = partial_total + local_sums(arrived[extra], have + extra)
        held = jnp.concatenate([held, arrived], axis=0)
    pieces = partial_total.reshape((replicas, -1) + partial_total.shape[1:])
    pieces = lax.all_to_all(pieces, "rep", 0, 0)
    edge_sums = jnp.sum(pieces, axis=0)
    share_rows = edge_sums.shape[0]
    share_start = replica * share_rows
    own_rows = lax.dynamic_slice_in_dim(scaled, share_start, share_rows, 0).astype(jnp.float32)
    own_inv = lax.dynamic_slice_in_dim(inv_deg, share_start, share_rows, 0)
    aggregate = (own_inv[:, None] * (edge_sums + own_rows)).astype(jnp.bfloat16)
    pre_act = jnp.dot(aggregate, weight, preferred_element_type=jnp.float32) + bias
    activated, pull_back = jax.vjp(gelu_tanh, pre_act)
    delta_bf = pull_back(cotangent.astype(jnp.float32))[0].astype(jnp.bfloat16)
    local_weight = lax.dot_general(
        aggregate, delta_bf, (((0,), (0,)), ((), ())), preferred_element_type=jnp.float32
    )
    local_bias = jnp.sum(delta_bf.astype(jnp.float32), axis=0)
    feat_rows = local_weight.shape[0]
    packed = jnp.concatenate(
        [local_weight, jnp.broadcast_to(local_bias[None, :], (8, local_bias.shape[0]))], axis=0
    )
    packed = butterfly_sum(packed, "rep", REP_BITS)
    packed = butterfly_sum(packed, "rows", ROWS_BITS)
    grad_weight = packed[:feat_rows]
    grad_bias = packed[feat_rows]
    return (activated.astype(jnp.bfloat16), grad_weight, grad_bias)


def solution(mesh):
    in_specs = (
        P("rows", None),
        P("rows"),
        P("rows", "rep", None),
        P("rows", "rep", None),
        P("rows", "rep", None, None),
        P(),
        P(),
        P(("rows", "rep"), None),
    )
    out_specs = (P(("rows", "rep"), None), P(), P())
    return jax.shard_map(local, mesh=mesh, in_specs=in_specs, out_specs=out_specs, check_vma=False)
```

```python
import jax
import jax.numpy as jnp
from jax import lax
from jax.experimental import pallas as pl
from jax.experimental.pallas import tpu as pltpu
from jax.sharding import PartitionSpec as P

ROWS_BITS = (0, 3, 1, 4, 2, 5)
REP_BITS = (0, 1, 2)


def from_behind(value, axis, steps):
    count = lax.axis_size(axis)
    pairs = [(source, (source + steps) % count) for source in range(count)]
    return lax.ppermute(value, axis, pairs)


def butterfly_sum(value, axis, order):
    count = lax.axis_size(axis)
    for bit in order:
        if (1 << bit) >= count:
            continue
        pairs = [(source, source ^ (1 << bit)) for source in range(count)]
        value = value + lax.ppermute(value, axis, pairs)
    return value


def halving_scatter(value, axis):
    count = lax.axis_size(axis)
    me = lax.axis_index(axis)
    levels = count.bit_length() - 1
    share = value.shape[0] // count
    buf = value.reshape((2,) * levels + (share,) + value.shape[1:])
    for bit in range(levels):
        dim = levels - 1 - bit
        mine = (me >> bit) & 1
        keep = lax.dynamic_index_in_dim(buf, mine, dim, keepdims=False)
        send = lax.dynamic_index_in_dim(buf, 1 - mine, dim, keepdims=False)
        pairs = [(source, source ^ (1 << bit)) for source in range(count)]
        buf = keep + lax.ppermute(send, axis, pairs)
    return buf


def gelu_tanh(values):
    return jax.nn.gelu(values, approximate=True)


def _edge_kernel(bufT_ref, far_ref, tgt_ref, out_ref):
    groups, feat, cols = bufT_ref.shape
    blocks, _, slots, edges = far_ref.shape
    col_iota = lax.broadcasted_iota(jnp.int32, (cols, edges), 0)
    row_iota = lax.broadcasted_iota(jnp.int32, (out_ref.shape[1], edges), 0)
    for b in range(blocks):
        acc = jnp.zeros((out_ref.shape[1], feat), jnp.float32)
        for g in range(groups):
            tableT = bufT_ref[g]
            for k in range(slots):
                far = far_ref[b, g, pl.ds(k, 1), :]
                tgt = tgt_ref[b, g, pl.ds(k, 1), :]
                pick = (col_iota == far).astype(jnp.bfloat16)
                pickedT = jnp.dot(tableT, pick, preferred_element_type=jnp.float32).astype(jnp.bfloat16)
                scatter = (row_iota == tgt).astype(jnp.bfloat16)
                acc = acc + lax.dot_general(
                    scatter, pickedT, (((1,), (1,)), ((), ())), preferred_element_type=jnp.float32
                )
        out_ref[b] = acc


def edge_sums_kernel(bufT, far, tgt):
    groups, feat, cols = bufT.shape
    blocks = far.shape[0]
    rows = 128
    flops = 2 * blocks * groups * far.shape[2] * (feat * cols * 128 + rows * 128 * feat)
    return pl.pallas_call(
        _edge_kernel,
        out_shape=jax.ShapeDtypeStruct((blocks, rows, feat), jnp.float32),
        in_specs=[pl.BlockSpec(memory_space=pltpu.VMEM)] * 3,
        out_specs=pl.BlockSpec(memory_space=pltpu.VMEM),
        cost_estimate=pl.CostEstimate(
            flops=flops, transcendentals=0,
            bytes_accessed=bufT.size * 2 + far.size * 8 + blocks * rows * feat * 4,
        ),
    )(bufT, far, tgt)


def tile_sums(buffer, offset, tile_block, edge_count, edge_code):
    block_ids = lax.dynamic_index_in_dim(tile_block, offset, 1, keepdims=False)
    live_count = lax.dynamic_index_in_dim(edge_count, offset, 1, keepdims=False)
    codes = lax.dynamic_index_in_dim(edge_code, offset, 1, keepdims=False)
    block_total, slot_count, edge_cap = codes.shape
    feat_width = buffer.shape[1]
    far_node = block_ids[:, :, None] * 128 + codes % 128
    col_iota = lax.broadcasted_iota(jnp.int32, (1, 1, 1, buffer.shape[0]), 3)
    onehot_col = (far_node[..., None] == col_iota).astype(jnp.bfloat16)
    picked = jnp.einsum(
        "bkec,cf->bkef", onehot_col, buffer, preferred_element_type=jnp.float32
    ).astype(jnp.bfloat16)
    is_live = lax.broadcasted_iota(jnp.int32, codes.shape, 2) < live_count[:, :, None]
    target = jnp.where(is_live, codes // 128, -1)
    row_iota = lax.broadcasted_iota(jnp.int32, (1, 1, 128, 1), 2)
    onehot = (target[:, :, None, :] == row_iota).astype(jnp.bfloat16)
    summed = jnp.einsum("bkre,bkef->brf", onehot, picked, preferred_element_type=jnp.float32)
    return summed.reshape(block_total * 128, feat_width)


def local(features, degree, tile_block, edge_count, edge_code, weight, bias, cotangent):
    step_count = tile_block.shape[1]
    replicas = lax.axis_size("rep")
    replica = lax.axis_index("rep")
    inv_deg = lax.rsqrt(degree.astype(jnp.float32))
    scaled = (features.astype(jnp.float32) * inv_deg[:, None]).astype(jnp.bfloat16)

    far = tile_block[..., None] * 128 + edge_code % 128
    is_live = lax.broadcasted_iota(jnp.int32, edge_code.shape, 3) < edge_count[..., None]
    tgt = jnp.where(is_live, edge_code // 128, -1)

    def local_sums(held_t, first):
        count = held_t.shape[0]
        return edge_sums_kernel(held_t, far[:, first:first + count], tgt[:, first:first + count])

    row_count = lax.axis_size("rows")
    pairs = []
    for rep_index in range(replicas):
        for source in range(row_count):
            target = (source - step_count * rep_index) % row_count
            pairs.append((source * replicas + rep_index, target * replicas + rep_index))
    held = lax.ppermute(scaled.T, ("rows", "rep"), pairs)[None]
    partial_total = local_sums(held, 0)
    while held.shape[0] < step_count:
        have = held.shape[0]
        arrived = from_behind(held, "rows", -have)
        partial_total = partial_total + local_sums(arrived, have)
        held = jnp.concatenate([held, arrived], axis=0)
    partial_total = partial_total.reshape(-1, partial_total.shape[-1])
    pieces = partial_total.reshape((replicas, -1) + partial_total.shape[1:])
    pieces = lax.all_to_all(pieces, "rep", 0, 0)
    edge_sums = jnp.sum(pieces, axis=0)
    share_rows = edge_sums.shape[0]
    share_start = replica * share_rows
    own_rows = lax.dynamic_slice_in_dim(scaled, share_start, share_rows, 0).astype(jnp.float32)
    own_inv = lax.dynamic_slice_in_dim(inv_deg, share_start, share_rows, 0)
    aggregate = (own_inv[:, None] * (edge_sums + own_rows)).astype(jnp.bfloat16)
    pre_act = jnp.dot(aggregate, weight, preferred_element_type=jnp.float32) + bias
    activated, pull_back = jax.vjp(gelu_tanh, pre_act)
    delta_bf = pull_back(cotangent.astype(jnp.float32))[0].astype(jnp.bfloat16)
    local_weight = lax.dot_general(
        aggregate, delta_bf, (((0,), (0,)), ((), ())), preferred_element_type=jnp.float32
    )
    local_bias = jnp.sum(delta_bf.astype(jnp.float32), axis=0)
    feat_rows = local_weight.shape[0]
    packed = jnp.concatenate(
        [local_weight, jnp.broadcast_to(local_bias[None, :], (8, local_bias.shape[0]))], axis=0
    )
    packed = butterfly_sum(packed, "rep", REP_BITS)
    packed = butterfly_sum(packed, "rows", ROWS_BITS)
    grad_weight = packed[:feat_rows]
    grad_bias = packed[feat_rows]
    return (activated.astype(jnp.bfloat16), grad_weight, grad_bias)


def solution(mesh):
    in_specs = (
        P("rows", None),
        P("rows"),
        P("rows", "rep", None),
        P("rows", "rep", None),
        P("rows", "rep", None, None),
        P(),
        P(),
        P(("rows", "rep"), None),
    )
    out_specs = (P(("rows", "rep"), None), P(), P())
    return jax.shard_map(local, mesh=mesh, in_specs=in_specs, out_specs=out_specs, check_vma=False)
```

```python
import jax
import jax.numpy as jnp
from jax import lax
from jax.experimental import pallas as pl
from jax.experimental.pallas import tpu as pltpu
from jax.sharding import PartitionSpec as P

ROWS_BITS = (0, 3, 1, 4, 2, 5)
REP_BITS = (0, 1, 2)


def from_behind(value, axis, steps):
    count = lax.axis_size(axis)
    pairs = [(source, (source + steps) % count) for source in range(count)]
    return lax.ppermute(value, axis, pairs)


def butterfly_sum(value, axis, order):
    count = lax.axis_size(axis)
    for bit in order:
        if (1 << bit) >= count:
            continue
        pairs = [(source, source ^ (1 << bit)) for source in range(count)]
        value = value + lax.ppermute(value, axis, pairs)
    return value


def halving_scatter(value, axis):
    count = lax.axis_size(axis)
    me = lax.axis_index(axis)
    levels = count.bit_length() - 1
    share = value.shape[0] // count
    buf = value.reshape((2,) * levels + (share,) + value.shape[1:])
    for bit in range(levels):
        dim = levels - 1 - bit
        mine = (me >> bit) & 1
        keep = lax.dynamic_index_in_dim(buf, mine, dim, keepdims=False)
        send = lax.dynamic_index_in_dim(buf, 1 - mine, dim, keepdims=False)
        pairs = [(source, source ^ (1 << bit)) for source in range(count)]
        buf = keep + lax.ppermute(send, axis, pairs)
    return buf


def gelu_tanh(values):
    return jax.nn.gelu(values, approximate=True)


def _edge_kernel(bufT_ref, far_ref, tgt_ref, out_ref):
    groups, feat, cols = bufT_ref.shape
    blocks, _, slots, edges = far_ref.shape
    col_iota = lax.broadcasted_iota(jnp.int32, (cols, edges), 0)
    row_iota = lax.broadcasted_iota(jnp.int32, (out_ref.shape[1], edges), 0)
    for b in range(blocks):
        acc = jnp.zeros((out_ref.shape[1], feat), jnp.float32)
        for g in range(groups):
            far = far_ref[b, g]
            tgt = tgt_ref[b, g]
            pick = jnp.concatenate(
                [(col_iota == far[k:k + 1, :]).astype(jnp.bfloat16) for k in range(slots)], axis=1
            )
            scatter = jnp.concatenate(
                [(row_iota == tgt[k:k + 1, :]).astype(jnp.bfloat16) for k in range(slots)], axis=1
            )
            pickedT = jnp.dot(bufT_ref[g], pick, preferred_element_type=jnp.float32)
            acc = acc + lax.dot_general(
                scatter, pickedT.astype(jnp.bfloat16), (((1,), (1,)), ((), ())),
                preferred_element_type=jnp.float32,
            )
        out_ref[b] = acc


def edge_sums_kernel(bufT, far, tgt):
    groups, feat, cols = bufT.shape
    blocks = far.shape[0]
    rows = 128
    flops = 2 * blocks * groups * far.shape[2] * (feat * cols * 128 + rows * 128 * feat)
    return pl.pallas_call(
        _edge_kernel,
        out_shape=jax.ShapeDtypeStruct((blocks, rows, feat), jnp.float32),
        in_specs=[pl.BlockSpec(memory_space=pltpu.VMEM)] * 3,
        out_specs=pl.BlockSpec(memory_space=pltpu.VMEM),
        cost_estimate=pl.CostEstimate(
            flops=flops, transcendentals=0,
            bytes_accessed=bufT.size * 2 + far.size * 8 + blocks * rows * feat * 4,
        ),
    )(bufT, far, tgt)


def tile_sums(buffer, offset, tile_block, edge_count, edge_code):
    block_ids = lax.dynamic_index_in_dim(tile_block, offset, 1, keepdims=False)
    live_count = lax.dynamic_index_in_dim(edge_count, offset, 1, keepdims=False)
    codes = lax.dynamic_index_in_dim(edge_code, offset, 1, keepdims=False)
    block_total, slot_count, edge_cap = codes.shape
    feat_width = buffer.shape[1]
    far_node = block_ids[:, :, None] * 128 + codes % 128
    col_iota = lax.broadcasted_iota(jnp.int32, (1, 1, 1, buffer.shape[0]), 3)
    onehot_col = (far_node[..., None] == col_iota).astype(jnp.bfloat16)
    picked = jnp.einsum(
        "bkec,cf->bkef", onehot_col, buffer, preferred_element_type=jnp.float32
    ).astype(jnp.bfloat16)
    is_live = lax.broadcasted_iota(jnp.int32, codes.shape, 2) < live_count[:, :, None]
    target = jnp.where(is_live, codes // 128, -1)
    row_iota = lax.broadcasted_iota(jnp.int32, (1, 1, 128, 1), 2)
    onehot = (target[:, :, None, :] == row_iota).astype(jnp.bfloat16)
    summed = jnp.einsum("bkre,bkef->brf", onehot, picked, preferred_element_type=jnp.float32)
    return summed.reshape(block_total * 128, feat_width)


def local(features, degree, tile_block, edge_count, edge_code, weight, bias, cotangent):
    step_count = tile_block.shape[1]
    replicas = lax.axis_size("rep")
    replica = lax.axis_index("rep")
    inv_deg = lax.rsqrt(degree.astype(jnp.float32))
    scaled = (features.astype(jnp.float32) * inv_deg[:, None]).astype(jnp.bfloat16)

    far = tile_block[..., None] * 128 + edge_code % 128
    is_live = lax.broadcasted_iota(jnp.int32, edge_code.shape, 3) < edge_count[..., None]
    tgt = jnp.where(is_live, edge_code // 128, -1)

    def local_sums(held_t, first):
        count = held_t.shape[0]
        return edge_sums_kernel(held_t, far[:, first:first + count], tgt[:, first:first + count])

    row_count = lax.axis_size("rows")
    pairs = []
    for rep_index in range(replicas):
        for source in range(row_count):
            target = (source - step_count * rep_index) % row_count
            pairs.append((source * replicas + rep_index, target * replicas + rep_index))
    held = lax.ppermute(scaled.T, ("rows", "rep"), pairs)[None]
    partial_total = local_sums(held, 0)
    while held.shape[0] < step_count:
        have = held.shape[0]
        arrived = from_behind(held, "rows", -have)
        partial_total = partial_total + local_sums(arrived, have)
        held = jnp.concatenate([held, arrived], axis=0)
    partial_total = partial_total.reshape(-1, partial_total.shape[-1])
    pieces = partial_total.reshape((replicas, -1) + partial_total.shape[1:])
    pieces = lax.all_to_all(pieces, "rep", 0, 0)
    edge_sums = jnp.sum(pieces, axis=0)
    share_rows = edge_sums.shape[0]
    share_start = replica * share_rows
    own_rows = lax.dynamic_slice_in_dim(scaled, share_start, share_rows, 0).astype(jnp.float32)
    own_inv = lax.dynamic_slice_in_dim(inv_deg, share_start, share_rows, 0)
    aggregate = (own_inv[:, None] * (edge_sums + own_rows)).astype(jnp.bfloat16)
    pre_act = jnp.dot(aggregate, weight, preferred_element_type=jnp.float32) + bias
    activated, pull_back = jax.vjp(gelu_tanh, pre_act)
    delta_bf = pull_back(cotangent.astype(jnp.float32))[0].astype(jnp.bfloat16)
    local_weight = lax.dot_general(
        aggregate, delta_bf, (((0,), (0,)), ((), ())), preferred_element_type=jnp.float32
    )
    local_bias = jnp.sum(delta_bf.astype(jnp.float32), axis=0)
    feat_rows = local_weight.shape[0]
    packed = jnp.concatenate(
        [local_weight, jnp.broadcast_to(local_bias[None, :], (8, local_bias.shape[0]))], axis=0
    )
    packed = butterfly_sum(packed, "rep", REP_BITS)
    packed = butterfly_sum(packed, "rows", ROWS_BITS)
    grad_weight = packed[:feat_rows]
    grad_bias = packed[feat_rows]
    return (activated.astype(jnp.bfloat16), grad_weight, grad_bias)


def solution(mesh):
    in_specs = (
        P("rows", None),
        P("rows"),
        P("rows", "rep", None),
        P("rows", "rep", None),
        P("rows", "rep", None, None),
        P(),
        P(),
        P(("rows", "rep"), None),
    )
    out_specs = (P(("rows", "rep"), None), P(), P())
    return jax.shard_map(local, mesh=mesh, in_specs=in_specs, out_specs=out_specs, check_vma=False)
```

```python
import jax
import jax.numpy as jnp
from jax import lax
from jax.experimental import pallas as pl
from jax.experimental.pallas import tpu as pltpu
from jax.sharding import PartitionSpec as P

ROWS_BITS = (0, 3, 1, 4, 2, 5)
REP_BITS = (0, 1, 2)


def from_behind(value, axis, steps):
    count = lax.axis_size(axis)
    pairs = [(source, (source + steps) % count) for source in range(count)]
    return lax.ppermute(value, axis, pairs)


def butterfly_sum(value, axis, order):
    count = lax.axis_size(axis)
    for bit in order:
        if (1 << bit) >= count:
            continue
        pairs = [(source, source ^ (1 << bit)) for source in range(count)]
        value = value + lax.ppermute(value, axis, pairs)
    return value


def halving_scatter(value, axis):
    count = lax.axis_size(axis)
    me = lax.axis_index(axis)
    levels = count.bit_length() - 1
    share = value.shape[0] // count
    buf = value.reshape((2,) * levels + (share,) + value.shape[1:])
    for bit in range(levels):
        dim = levels - 1 - bit
        mine = (me >> bit) & 1
        keep = lax.dynamic_index_in_dim(buf, mine, dim, keepdims=False)
        send = lax.dynamic_index_in_dim(buf, 1 - mine, dim, keepdims=False)
        pairs = [(source, source ^ (1 << bit)) for source in range(count)]
        buf = keep + lax.ppermute(send, axis, pairs)
    return buf


def gelu_tanh(values):
    return jax.nn.gelu(values, approximate=True)


def _edge_kernel(bufT_ref, far_ref, tgt_ref, out_ref):
    groups, feat, cols = bufT_ref.shape
    blocks, _, slots, edges = far_ref.shape
    col_iota = lax.broadcasted_iota(jnp.int32, (cols, edges), 0)
    row_iota = lax.broadcasted_iota(jnp.int32, (out_ref.shape[1], edges), 0)
    for b in range(blocks):
        acc = jnp.zeros((out_ref.shape[1], feat), jnp.float32)
        for g in range(groups):
            far = far_ref[b, g]
            tgt = tgt_ref[b, g]
            pick = jnp.concatenate(
                [(col_iota == far[k:k + 1, :]).astype(jnp.bfloat16) for k in range(slots)], axis=1
            )
            scatter = jnp.concatenate(
                [(row_iota == tgt[k:k + 1, :]).astype(jnp.bfloat16) for k in range(slots)], axis=1
            )
            pickedT = jnp.dot(bufT_ref[g], pick, preferred_element_type=jnp.float32)
            acc = acc + lax.dot_general(
                scatter, pickedT.astype(jnp.bfloat16), (((1,), (1,)), ((), ())),
                preferred_element_type=jnp.float32,
            )
        out_ref[b] = acc


def edge_sums_kernel(bufT, far, tgt):
    groups, feat, cols = bufT.shape
    blocks = far.shape[0]
    rows = 128
    flops = 2 * blocks * groups * far.shape[2] * (feat * cols * 128 + rows * 128 * feat)
    return pl.pallas_call(
        _edge_kernel,
        out_shape=jax.ShapeDtypeStruct((blocks, rows, feat), jnp.float32),
        in_specs=[pl.BlockSpec(memory_space=pltpu.VMEM)] * 3,
        out_specs=pl.BlockSpec(memory_space=pltpu.VMEM),
        cost_estimate=pl.CostEstimate(
            flops=flops, transcendentals=0,
            bytes_accessed=bufT.size * 2 + far.size * 8 + blocks * rows * feat * 4,
        ),
    )(bufT, far, tgt)


def tile_sums(buffer, offset, tile_block, edge_count, edge_code):
    block_ids = lax.dynamic_index_in_dim(tile_block, offset, 1, keepdims=False)
    live_count = lax.dynamic_index_in_dim(edge_count, offset, 1, keepdims=False)
    codes = lax.dynamic_index_in_dim(edge_code, offset, 1, keepdims=False)
    block_total, slot_count, edge_cap = codes.shape
    feat_width = buffer.shape[1]
    far_node = block_ids[:, :, None] * 128 + codes % 128
    col_iota = lax.broadcasted_iota(jnp.int32, (1, 1, 1, buffer.shape[0]), 3)
    onehot_col = (far_node[..., None] == col_iota).astype(jnp.bfloat16)
    picked = jnp.einsum(
        "bkec,cf->bkef", onehot_col, buffer, preferred_element_type=jnp.float32
    ).astype(jnp.bfloat16)
    is_live = lax.broadcasted_iota(jnp.int32, codes.shape, 2) < live_count[:, :, None]
    target = jnp.where(is_live, codes // 128, -1)
    row_iota = lax.broadcasted_iota(jnp.int32, (1, 1, 128, 1), 2)
    onehot = (target[:, :, None, :] == row_iota).astype(jnp.bfloat16)
    summed = jnp.einsum("bkre,bkef->brf", onehot, picked, preferred_element_type=jnp.float32)
    return summed.reshape(block_total * 128, feat_width)


def local(features, degree, tile_block, edge_count, edge_code, weight, bias, cotangent):
    step_count = tile_block.shape[1]
    replicas = lax.axis_size("rep")
    replica = lax.axis_index("rep")
    inv_deg = lax.rsqrt(degree.astype(jnp.float32))
    scaled = (features.astype(jnp.float32) * inv_deg[:, None]).astype(jnp.bfloat16)

    far = tile_block[..., None] * 128 + edge_code % 128
    is_live = lax.broadcasted_iota(jnp.int32, edge_code.shape, 3) < edge_count[..., None]
    tgt = jnp.where(is_live, edge_code // 128, -1)

    def local_sums(held_t, chosen):
        index = jnp.array(chosen, jnp.int32)
        return edge_sums_kernel(held_t, far[:, index], tgt[:, index])

    row_count = lax.axis_size("rows")
    pairs = []
    for rep_index in range(replicas):
        for source in range(row_count):
            target = (source - step_count * rep_index) % row_count
            pairs.append((source * replicas + rep_index, target * replicas + rep_index))
    held = lax.ppermute(scaled.T, ("rows", "rep"), pairs)[None]
    offsets = [0]
    partial_total = local_sums(held, offsets)
    stride = step_count
    while stride > 1:
        stride //= 2
        arrived = from_behind(held, "rows", -stride)
        arrived_offsets = [offset + stride for offset in offsets]
        partial_total = partial_total + local_sums(arrived, arrived_offsets)
        held = jnp.concatenate([held, arrived], axis=0)
        offsets = offsets + arrived_offsets
    partial_total = partial_total.reshape(-1, partial_total.shape[-1])
    pieces = partial_total.reshape((replicas, -1) + partial_total.shape[1:])
    pieces = lax.all_to_all(pieces, "rep", 0, 0)
    edge_sums = jnp.sum(pieces, axis=0)
    share_rows = edge_sums.shape[0]
    share_start = replica * share_rows
    own_rows = lax.dynamic_slice_in_dim(scaled, share_start, share_rows, 0).astype(jnp.float32)
    own_inv = lax.dynamic_slice_in_dim(inv_deg, share_start, share_rows, 0)
    aggregate = (own_inv[:, None] * (edge_sums + own_rows)).astype(jnp.bfloat16)
    pre_act = jnp.dot(aggregate, weight, preferred_element_type=jnp.float32) + bias
    activated, pull_back = jax.vjp(gelu_tanh, pre_act)
    delta_bf = pull_back(cotangent.astype(jnp.float32))[0].astype(jnp.bfloat16)
    local_weight = lax.dot_general(
        aggregate, delta_bf, (((0,), (0,)), ((), ())), preferred_element_type=jnp.float32
    )
    local_bias = jnp.sum(delta_bf.astype(jnp.float32), axis=0)
    feat_rows = local_weight.shape[0]
    packed = jnp.concatenate(
        [local_weight, jnp.broadcast_to(local_bias[None, :], (8, local_bias.shape[0]))], axis=0
    )
    packed = butterfly_sum(packed, "rep", REP_BITS)
    packed = butterfly_sum(packed, "rows", ROWS_BITS)
    grad_weight = packed[:feat_rows]
    grad_bias = packed[feat_rows]
    return (activated.astype(jnp.bfloat16), grad_weight, grad_bias)


def solution(mesh):
    in_specs = (
        P("rows", None),
        P("rows"),
        P("rows", "rep", None),
        P("rows", "rep", None),
        P("rows", "rep", None, None),
        P(),
        P(),
        P(("rows", "rep"), None),
    )
    out_specs = (P(("rows", "rep"), None), P(), P())
    return jax.shard_map(local, mesh=mesh, in_specs=in_specs, out_specs=out_specs, check_vma=False)
```

```python
import jax
import jax.numpy as jnp
from jax import lax
from jax.experimental import pallas as pl
from jax.experimental.pallas import tpu as pltpu
from jax.sharding import PartitionSpec as P


ROWS_BITS = (0, 3, 1, 4, 2, 5)


def from_behind(value, axis, steps):
    count = lax.axis_size(axis)
    pairs = [(source, (source + steps) % count) for source in range(count)]
    return lax.ppermute(value, axis, pairs)


def butterfly_sum(value, axis, order):
    count = lax.axis_size(axis)
    for bit in order:
        if (1 << bit) >= count:
            continue
        pairs = [(source, source ^ (1 << bit)) for source in range(count)]
        value = value + lax.ppermute(value, axis, pairs)
    return value


def gelu_tanh(values):
    return jax.nn.gelu(values, approximate=True)


def _edge_kernel(bufT_ref, far_ref, tgt_ref, out_ref):
    groups, feat, cols = bufT_ref.shape
    blocks, _, slots, edges = far_ref.shape
    col_iota = lax.broadcasted_iota(jnp.int32, (cols, edges), 0)
    row_iota = lax.broadcasted_iota(jnp.int32, (out_ref.shape[1], edges), 0)
    for b in range(blocks):
        acc = jnp.zeros((out_ref.shape[1], feat), jnp.float32)
        for g in range(groups):
            far = far_ref[b, g]
            tgt = tgt_ref[b, g]
            pick = jnp.concatenate(
                [(col_iota == far[k:k + 1, :]).astype(jnp.bfloat16) for k in range(slots)], axis=1
            )
            scatter = jnp.concatenate(
                [(row_iota == tgt[k:k + 1, :]).astype(jnp.bfloat16) for k in range(slots)], axis=1
            )
            pickedT = jnp.dot(bufT_ref[g], pick, preferred_element_type=jnp.float32)
            acc = acc + lax.dot_general(
                scatter, pickedT.astype(jnp.bfloat16), (((1,), (1,)), ((), ())),
                preferred_element_type=jnp.float32,
            )
        out_ref[b] = acc


def edge_sums_kernel(bufT, far, tgt):
    groups, feat, cols = bufT.shape
    blocks = far.shape[0]
    rows = 128
    flops = 2 * blocks * groups * far.shape[2] * (feat * cols * 128 + rows * 128 * feat)
    return pl.pallas_call(
        _edge_kernel,
        out_shape=jax.ShapeDtypeStruct((blocks, rows, feat), jnp.float32),
        in_specs=[pl.BlockSpec(memory_space=pltpu.VMEM)] * 3,
        out_specs=pl.BlockSpec(memory_space=pltpu.VMEM),
        cost_estimate=pl.CostEstimate(
            flops=flops, transcendentals=0,
            bytes_accessed=bufT.size * 2 + far.size * 8 + blocks * rows * feat * 4,
        ),
    )(bufT, far, tgt)


def layer(features, degree, tile_block, edge_count, edge_code, weight, bias, cotangent):
    step_count = tile_block.shape[1]
    replicas = lax.axis_size("rep")
    replica = lax.axis_index("rep")
    inv_deg = lax.rsqrt(degree.astype(jnp.float32))
    scaled = (features.astype(jnp.float32) * inv_deg[:, None]).astype(jnp.bfloat16)

    far = tile_block[..., None] * 128 + edge_code % 128
    is_live = lax.broadcasted_iota(jnp.int32, edge_code.shape, 3) < edge_count[..., None]
    tgt = jnp.where(is_live, edge_code // 128, -1)

    def local_sums(held_t, chosen):
        index = jnp.array(chosen, jnp.int32)
        return edge_sums_kernel(held_t, far[:, index], tgt[:, index])

    row_count = lax.axis_size("rows")
    pairs = []
    for rep_index in range(replicas):
        for source in range(row_count):
            target = (source - step_count * rep_index) % row_count
            pairs.append((source * replicas + rep_index, target * replicas + rep_index))
    held = lax.ppermute(scaled.T, ("rows", "rep"), pairs)[None]
    cot_copies = jnp.broadcast_to(cotangent[None], (replicas,) + cotangent.shape)
    cot_group = lax.all_to_all(cot_copies, "rep", 0, 0).reshape(-1, cotangent.shape[1])
    offsets = [0]
    partial_total = local_sums(held, offsets)
    stride = step_count
    while stride > 1:
        stride //= 2
        arrived = from_behind(held, "rows", -stride)
        arrived_offsets = [offset + stride for offset in offsets]
        partial_total = partial_total + local_sums(arrived, arrived_offsets)
        held = jnp.concatenate([held, arrived], axis=0)
        offsets = offsets + arrived_offsets
    partial_total = partial_total.reshape(-1, partial_total.shape[-1])
    pieces = partial_total.reshape((replicas, -1) + partial_total.shape[1:])
    pieces = lax.all_to_all(pieces, "rep", 0, 0)
    share = jnp.sum(pieces, axis=0)
    copies = jnp.broadcast_to(share[None], (replicas,) + share.shape)
    edge_sums = lax.all_to_all(copies, "rep", 0, 0).reshape(partial_total.shape)
    aggregate = (inv_deg[:, None] * (edge_sums + scaled.astype(jnp.float32))).astype(jnp.bfloat16)
    pre_act = jnp.dot(aggregate, weight, preferred_element_type=jnp.float32) + bias
    activated, pull_back = jax.vjp(gelu_tanh, pre_act)
    delta_bf = pull_back(cot_group.astype(jnp.float32))[0].astype(jnp.bfloat16)
    local_weight = lax.dot_general(
        aggregate, delta_bf, (((0,), (0,)), ((), ())), preferred_element_type=jnp.float32
    )
    local_bias = jnp.sum(delta_bf.astype(jnp.float32), axis=0)
    feat_rows = local_weight.shape[0]
    packed = jnp.concatenate(
        [local_weight, jnp.broadcast_to(local_bias[None, :], (8, local_bias.shape[0]))], axis=0
    )
    packed = butterfly_sum(packed, "rows", ROWS_BITS)
    grad_weight = packed[:feat_rows]
    grad_bias = packed[feat_rows]
    share_rows = cotangent.shape[0]
    own_act = lax.dynamic_slice_in_dim(activated, replica * share_rows, share_rows, 0)
    return (own_act.astype(jnp.bfloat16), grad_weight, grad_bias)


def solution(mesh):
    in_specs = (
        P("rows", None),
        P("rows"),
        P("rows", "rep", None),
        P("rows", "rep", None),
        P("rows", "rep", None, None),
        P(),
        P(),
        P(("rows", "rep"), None),
    )
    out_specs = (P(("rows", "rep"), None), P(), P())
    return jax.shard_map(layer, mesh=mesh, in_specs=in_specs, out_specs=out_specs, check_vma=False)
```

```python
import jax
import jax.numpy as jnp
from jax import lax
from jax.experimental import pallas as pl
from jax.experimental.pallas import tpu as pltpu
from jax.sharding import PartitionSpec as P


def from_behind(value, axis, steps):
    count = lax.axis_size(axis)
    pairs = [(source, (source + steps) % count) for source in range(count)]
    return lax.ppermute(value, axis, pairs)


def quad_sum(value, axis, bit_pairs):
    count = lax.axis_size(axis)
    me = lax.axis_index(axis)
    for low, high in bit_pairs:
        masks = (1 << low, 1 << high, (1 << low) | (1 << high))
        got = {0: value}
        for mask in masks:
            pairs = [(source, source ^ mask) for source in range(count)]
            got[mask] = lax.ppermute(value, axis, pairs)
        lo_bit = (me >> low) & 1
        hi_bit = (me >> high) & 1
        terms = {}
        for mask, term in got.items():
            slot_lo = lo_bit ^ ((mask >> low) & 1)
            slot_hi = hi_bit ^ ((mask >> high) & 1)
            terms[mask] = (slot_lo, slot_hi, term)
        ordered = [None] * 4
        for position in range(4):
            want_lo, want_hi = position & 1, position >> 1
            pick = None
            for slot_lo, slot_hi, term in terms.values():
                hit = (slot_lo == want_lo) & (slot_hi == want_hi)
                pick = term if pick is None else jnp.where(hit, term, pick)
            ordered[position] = pick
        value = (ordered[0] + ordered[1]) + (ordered[2] + ordered[3])
    return value


def gelu_tanh(values):
    return jax.nn.gelu(values, approximate=True)


def _edge_kernel(bufT_ref, far_ref, tgt_ref, out_ref):
    groups, feat, cols = bufT_ref.shape
    blocks, _, slots, edges = far_ref.shape
    col_iota = lax.broadcasted_iota(jnp.int32, (cols, edges), 0)
    row_iota = lax.broadcasted_iota(jnp.int32, (out_ref.shape[1], edges), 0)
    for b in range(blocks):
        acc = jnp.zeros((out_ref.shape[1], feat), jnp.float32)
        for g in range(groups):
            far = far_ref[b, g]
            tgt = tgt_ref[b, g]
            pick = jnp.concatenate(
                [(col_iota == far[k:k + 1, :]).astype(jnp.bfloat16) for k in range(slots)], axis=1
            )
            scatter = jnp.concatenate(
                [(row_iota == tgt[k:k + 1, :]).astype(jnp.bfloat16) for k in range(slots)], axis=1
            )
            pickedT = jnp.dot(bufT_ref[g], pick, preferred_element_type=jnp.float32)
            acc = acc + lax.dot_general(
                scatter, pickedT.astype(jnp.bfloat16), (((1,), (1,)), ((), ())),
                preferred_element_type=jnp.float32,
            )
        out_ref[b] = acc


def edge_sums_kernel(bufT, far, tgt):
    groups, feat, cols = bufT.shape
    blocks = far.shape[0]
    rows = 128
    flops = 2 * blocks * groups * far.shape[2] * (feat * cols * 128 + rows * 128 * feat)
    return pl.pallas_call(
        _edge_kernel,
        out_shape=jax.ShapeDtypeStruct((blocks, rows, feat), jnp.float32),
        in_specs=[pl.BlockSpec(memory_space=pltpu.VMEM)] * 3,
        out_specs=pl.BlockSpec(memory_space=pltpu.VMEM),
        cost_estimate=pl.CostEstimate(
            flops=flops, transcendentals=0,
            bytes_accessed=bufT.size * 2 + far.size * 8 + blocks * rows * feat * 4,
        ),
    )(bufT, far, tgt)


def layer(features, degree, tile_block, edge_count, edge_code, weight, bias, cotangent):
    step_count = tile_block.shape[1]
    replicas = lax.axis_size("rep")
    replica = lax.axis_index("rep")
    inv_deg = lax.rsqrt(degree.astype(jnp.float32))
    scaled = (features.astype(jnp.float32) * inv_deg[:, None]).astype(jnp.bfloat16)

    far = tile_block[..., None] * 128 + edge_code % 128
    is_live = lax.broadcasted_iota(jnp.int32, edge_code.shape, 3) < edge_count[..., None]
    tgt = jnp.where(is_live, edge_code // 128, -1)

    def local_sums(held_t, chosen):
        index = jnp.array(chosen, jnp.int32)
        return edge_sums_kernel(held_t, far[:, index], tgt[:, index])

    row_count = lax.axis_size("rows")
    pairs = []
    for rep_index in range(replicas):
        for source in range(row_count):
            target = (source - step_count * rep_index) % row_count
            pairs.append((source * replicas + rep_index, target * replicas + rep_index))
    held = lax.ppermute(scaled.T, ("rows", "rep"), pairs)[None]
    cot_copies = jnp.broadcast_to(cotangent[None], (replicas,) + cotangent.shape)
    cot_group = lax.all_to_all(cot_copies, "rep", 0, 0).reshape(-1, cotangent.shape[1])
    offsets = [0]
    partial_total = local_sums(held, offsets)
    stride = step_count
    while stride > 1:
        stride //= 2
        arrived = from_behind(held, "rows", -stride)
        arrived_offsets = [offset + stride for offset in offsets]
        partial_total = partial_total + local_sums(arrived, arrived_offsets)
        held = jnp.concatenate([held, arrived], axis=0)
        offsets = offsets + arrived_offsets
    partial_total = partial_total.reshape(-1, partial_total.shape[-1])
    pieces = partial_total.reshape((replicas, -1) + partial_total.shape[1:])
    pieces = lax.all_to_all(pieces, "rep", 0, 0)
    share = jnp.sum(pieces, axis=0)
    copies = jnp.broadcast_to(share[None], (replicas,) + share.shape)
    edge_sums = lax.all_to_all(copies, "rep", 0, 0).reshape(partial_total.shape)
    aggregate = (inv_deg[:, None] * (edge_sums + scaled.astype(jnp.float32))).astype(jnp.bfloat16)
    pre_act = jnp.dot(aggregate, weight, preferred_element_type=jnp.float32) + bias
    activated, pull_back = jax.vjp(gelu_tanh, pre_act)
    delta_bf = pull_back(cot_group.astype(jnp.float32))[0].astype(jnp.bfloat16)
    local_weight = lax.dot_general(
        aggregate, delta_bf, (((0,), (0,)), ((), ())), preferred_element_type=jnp.float32
    )
    local_bias = jnp.sum(delta_bf.astype(jnp.float32), axis=0)
    feat_rows = local_weight.shape[0]
    packed = jnp.concatenate(
        [local_weight, jnp.broadcast_to(local_bias[None, :], (8, local_bias.shape[0]))], axis=0
    )
    packed = quad_sum(packed, "rows", ((0, 3), (1, 4), (2, 5)))
    grad_weight = packed[:feat_rows]
    grad_bias = packed[feat_rows]
    share_rows = cotangent.shape[0]
    own_act = lax.dynamic_slice_in_dim(activated, replica * share_rows, share_rows, 0)
    return (own_act.astype(jnp.bfloat16), grad_weight, grad_bias)


def solution(mesh):
    in_specs = (
        P("rows", None),
        P("rows"),
        P("rows", "rep", None),
        P("rows", "rep", None),
        P("rows", "rep", None, None),
        P(),
        P(),
        P(("rows", "rep"), None),
    )
    out_specs = (P(("rows", "rep"), None), P(), P())
    return jax.shard_map(layer, mesh=mesh, in_specs=in_specs, out_specs=out_specs, check_vma=False)
```

```python
import jax
import jax.numpy as jnp
from jax import lax
from jax.experimental import pallas as pl
from jax.experimental.pallas import tpu as pltpu
from jax.sharding import PartitionSpec as P


ROWS_BITS = (0, 3, 1, 4, 2, 5)


def from_behind(value, axis, steps):
    count = lax.axis_size(axis)
    pairs = [(source, (source + steps) % count) for source in range(count)]
    return lax.ppermute(value, axis, pairs)


def butterfly_sum(value, axis, order):
    count = lax.axis_size(axis)
    for bit in order:
        if (1 << bit) >= count:
            continue
        pairs = [(source, source ^ (1 << bit)) for source in range(count)]
        value = value + lax.ppermute(value, axis, pairs)
    return value


def gelu_tanh(values):
    return jax.nn.gelu(values, approximate=True)


def _edge_kernel(bufT_ref, far_ref, tgt_ref, out_ref):
    groups, feat, cols = bufT_ref.shape
    blocks, _, slots, edges = far_ref.shape
    col_iota = lax.broadcasted_iota(jnp.int32, (cols, edges), 0)
    row_iota = lax.broadcasted_iota(jnp.int32, (out_ref.shape[1], edges), 0)
    for b in range(blocks):
        acc = jnp.zeros((out_ref.shape[1], feat), jnp.float32)
        for g in range(groups):
            far = far_ref[b, g]
            tgt = tgt_ref[b, g]
            pick = jnp.concatenate(
                [(col_iota == far[k:k + 1, :]).astype(jnp.bfloat16) for k in range(slots)], axis=1
            )
            scatter = jnp.concatenate(
                [(row_iota == tgt[k:k + 1, :]).astype(jnp.bfloat16) for k in range(slots)], axis=1
            )
            pickedT = jnp.dot(bufT_ref[g], pick, preferred_element_type=jnp.float32)
            acc = acc + lax.dot_general(
                scatter, pickedT.astype(jnp.bfloat16), (((1,), (1,)), ((), ())),
                preferred_element_type=jnp.float32,
            )
        out_ref[b] = acc


def edge_sums_kernel(bufT, far, tgt):
    groups, feat, cols = bufT.shape
    blocks = far.shape[0]
    rows = 128
    flops = 2 * blocks * groups * far.shape[2] * (feat * cols * 128 + rows * 128 * feat)
    return pl.pallas_call(
        _edge_kernel,
        out_shape=jax.ShapeDtypeStruct((blocks, rows, feat), jnp.float32),
        in_specs=[pl.BlockSpec(memory_space=pltpu.VMEM)] * 3,
        out_specs=pl.BlockSpec(memory_space=pltpu.VMEM),
        cost_estimate=pl.CostEstimate(
            flops=flops, transcendentals=0,
            bytes_accessed=bufT.size * 2 + far.size * 8 + blocks * rows * feat * 4,
        ),
    )(bufT, far, tgt)


def layer(features, degree, tile_block, edge_count, edge_code, weight, bias, cotangent):
    step_count = tile_block.shape[1]
    replicas = lax.axis_size("rep")
    replica = lax.axis_index("rep")
    inv_deg = lax.rsqrt(degree.astype(jnp.float32))
    scaled = (features.astype(jnp.float32) * inv_deg[:, None]).astype(jnp.bfloat16)

    far = tile_block[..., None] * 128 + edge_code % 128
    is_live = lax.broadcasted_iota(jnp.int32, edge_code.shape, 3) < edge_count[..., None]
    tgt = jnp.where(is_live, edge_code // 128, -1)

    def local_sums(held_t, chosen):
        index = jnp.array(chosen, jnp.int32)
        return edge_sums_kernel(held_t, far[:, index], tgt[:, index])

    row_count = lax.axis_size("rows")
    pairs = []
    for rep_index in range(replicas):
        for source in range(row_count):
            target = (source - step_count * rep_index) % row_count
            pairs.append((source * replicas + rep_index, target * replicas + rep_index))
    held = lax.ppermute(scaled.T, ("rows", "rep"), pairs)[None]
    offsets = [0]
    partial_total = local_sums(held, offsets)
    stride = step_count
    while stride > 1:
        stride //= 2
        arrived = from_behind(held, "rows", -stride)
        arrived_offsets = [offset + stride for offset in offsets]
        partial_total = partial_total + local_sums(arrived, arrived_offsets)
        held = jnp.concatenate([held, arrived], axis=0)
        offsets = offsets + arrived_offsets
    partial_total = partial_total.reshape(-1, partial_total.shape[-1])
    pieces = partial_total.reshape((replicas, -1) + partial_total.shape[1:])
    cot_copies = jnp.broadcast_to(
        cotangent.astype(jnp.float32)[None], (replicas,) + cotangent.shape
    )
    feat_width = pieces.shape[-1]
    pieces = lax.all_to_all(jnp.concatenate([pieces, cot_copies], axis=-1), "rep", 0, 0)
    share = jnp.sum(pieces[..., :feat_width], axis=0)
    cot_group = pieces[..., feat_width:].reshape(-1, cotangent.shape[1])
    copies = jnp.broadcast_to(share[None], (replicas,) + share.shape)
    edge_sums = lax.all_to_all(copies, "rep", 0, 0).reshape(partial_total.shape)
    aggregate = (inv_deg[:, None] * (edge_sums + scaled.astype(jnp.float32))).astype(jnp.bfloat16)
    pre_act = jnp.dot(aggregate, weight, preferred_element_type=jnp.float32) + bias
    activated, pull_back = jax.vjp(gelu_tanh, pre_act)
    delta_bf = pull_back(cot_group)[0].astype(jnp.bfloat16)
    local_weight = lax.dot_general(
        aggregate, delta_bf, (((0,), (0,)), ((), ())), preferred_element_type=jnp.float32
    )
    local_bias = jnp.sum(delta_bf.astype(jnp.float32), axis=0)
    feat_rows = local_weight.shape[0]
    packed = jnp.concatenate(
        [local_weight, jnp.broadcast_to(local_bias[None, :], (8, local_bias.shape[0]))], axis=0
    )
    packed = butterfly_sum(packed, "rows", ROWS_BITS)
    grad_weight = packed[:feat_rows]
    grad_bias = packed[feat_rows]
    share_rows = cotangent.shape[0]
    own_act = lax.dynamic_slice_in_dim(activated, replica * share_rows, share_rows, 0)
    return (own_act.astype(jnp.bfloat16), grad_weight, grad_bias)


def solution(mesh):
    in_specs = (
        P("rows", None),
        P("rows"),
        P("rows", "rep", None),
        P("rows", "rep", None),
        P("rows", "rep", None, None),
        P(),
        P(),
        P(("rows", "rep"), None),
    )
    out_specs = (P(("rows", "rep"), None), P(), P())
    return jax.shard_map(layer, mesh=mesh, in_specs=in_specs, out_specs=out_specs, check_vma=False)
```

```python
import jax
import jax.numpy as jnp
from jax import lax
from jax.experimental import pallas as pl
from jax.experimental.pallas import tpu as pltpu
from jax.sharding import PartitionSpec as P


def from_behind(value, axis, steps):
    count = lax.axis_size(axis)
    pairs = [(source, (source + steps) % count) for source in range(count)]
    return lax.ppermute(value, axis, pairs)


def butterfly_sum(value, axis, order):
    count = lax.axis_size(axis)
    for bit in order:
        if (1 << bit) >= count:
            continue
        pairs = [(source, source ^ (1 << bit)) for source in range(count)]
        value = value + lax.ppermute(value, axis, pairs)
    return value


def split_sum(value, axis, outer_bits, inner_bits):
    me = lax.axis_index(axis)
    count = lax.axis_size(axis)
    buf = value.reshape((2,) * len(outer_bits) + (-1,) + value.shape[1:])
    for bit in outer_bits:
        mine = (me >> bit) & 1
        keep = lax.dynamic_index_in_dim(buf, mine, 0, keepdims=False)
        send = lax.dynamic_index_in_dim(buf, 1 - mine, 0, keepdims=False)
        pairs = [(source, source ^ (1 << bit)) for source in range(count)]
        buf = keep + lax.ppermute(send, axis, pairs)
    buf = butterfly_sum(buf, axis, inner_bits)
    for bit in reversed(outer_bits):
        mine = (me >> bit) & 1
        pairs = [(source, source ^ (1 << bit)) for source in range(count)]
        other = lax.ppermute(buf, axis, pairs)
        buf = jnp.where(mine == 0, jnp.stack([buf, other]), jnp.stack([other, buf]))
    return buf.reshape(value.shape)


def gelu_tanh(values):
    return jax.nn.gelu(values, approximate=True)


def _edge_kernel(bufT_ref, far_ref, tgt_ref, out_ref):
    groups, feat, cols = bufT_ref.shape
    blocks, _, slots, edges = far_ref.shape
    col_iota = lax.broadcasted_iota(jnp.int32, (cols, edges), 0)
    row_iota = lax.broadcasted_iota(jnp.int32, (out_ref.shape[1], edges), 0)
    for b in range(blocks):
        acc = jnp.zeros((out_ref.shape[1], feat), jnp.float32)
        for g in range(groups):
            far = far_ref[b, g]
            tgt = tgt_ref[b, g]
            pick = jnp.concatenate(
                [(col_iota == far[k:k + 1, :]).astype(jnp.bfloat16) for k in range(slots)], axis=1
            )
            scatter = jnp.concatenate(
                [(row_iota == tgt[k:k + 1, :]).astype(jnp.bfloat16) for k in range(slots)], axis=1
            )
            pickedT = jnp.dot(bufT_ref[g], pick, preferred_element_type=jnp.float32)
            acc = acc + lax.dot_general(
                scatter, pickedT.astype(jnp.bfloat16), (((1,), (1,)), ((), ())),
                preferred_element_type=jnp.float32,
            )
        out_ref[b] = acc


def edge_sums_kernel(bufT, far, tgt):
    groups, feat, cols = bufT.shape
    blocks = far.shape[0]
    rows = 128
    flops = 2 * blocks * groups * far.shape[2] * (feat * cols * 128 + rows * 128 * feat)
    return pl.pallas_call(
        _edge_kernel,
        out_shape=jax.ShapeDtypeStruct((blocks, rows, feat), jnp.float32),
        in_specs=[pl.BlockSpec(memory_space=pltpu.VMEM)] * 3,
        out_specs=pl.BlockSpec(memory_space=pltpu.VMEM),
        cost_estimate=pl.CostEstimate(
            flops=flops, transcendentals=0,
            bytes_accessed=bufT.size * 2 + far.size * 8 + blocks * rows * feat * 4,
        ),
    )(bufT, far, tgt)


def layer(features, degree, tile_block, edge_count, edge_code, weight, bias, cotangent):
    step_count = tile_block.shape[1]
    replicas = lax.axis_size("rep")
    replica = lax.axis_index("rep")
    inv_deg = lax.rsqrt(degree.astype(jnp.float32))
    scaled = (features.astype(jnp.float32) * inv_deg[:, None]).astype(jnp.bfloat16)

    far = tile_block[..., None] * 128 + edge_code % 128
    is_live = lax.broadcasted_iota(jnp.int32, edge_code.shape, 3) < edge_count[..., None]
    tgt = jnp.where(is_live, edge_code // 128, -1)

    def local_sums(held_t, chosen):
        index = jnp.array(chosen, jnp.int32)
        return edge_sums_kernel(held_t, far[:, index], tgt[:, index])

    row_count = lax.axis_size("rows")
    pairs = []
    for rep_index in range(replicas):
        for source in range(row_count):
            target = (source - step_count * rep_index) % row_count
            pairs.append((source * replicas + rep_index, target * replicas + rep_index))
    held = lax.ppermute(scaled.T, ("rows", "rep"), pairs)[None]
    offsets = [0]
    partial_total = local_sums(held, offsets)
    stride = step_count
    while stride > 1:
        stride //= 2
        arrived = from_behind(held, "rows", -stride)
        arrived_offsets = [offset + stride for offset in offsets]
        partial_total = partial_total + local_sums(arrived, arrived_offsets)
        held = jnp.concatenate([held, arrived], axis=0)
        offsets = offsets + arrived_offsets
    partial_total = partial_total.reshape(-1, partial_total.shape[-1])
    pieces = partial_total.reshape((replicas, -1) + partial_total.shape[1:])
    cot_copies = jnp.broadcast_to(
        cotangent.astype(jnp.float32)[None], (replicas,) + cotangent.shape
    )
    feat_width = pieces.shape[-1]
    pieces = lax.all_to_all(jnp.concatenate([pieces, cot_copies], axis=-1), "rep", 0, 0)
    share = jnp.sum(pieces[..., :feat_width], axis=0)
    cot_group = pieces[..., feat_width:].reshape(-1, cotangent.shape[1])
    copies = jnp.broadcast_to(share[None], (replicas,) + share.shape)
    edge_sums = lax.all_to_all(copies, "rep", 0, 0).reshape(partial_total.shape)
    aggregate = (inv_deg[:, None] * (edge_sums + scaled.astype(jnp.float32))).astype(jnp.bfloat16)
    pre_act = jnp.dot(aggregate, weight, preferred_element_type=jnp.float32) + bias
    activated, pull_back = jax.vjp(gelu_tanh, pre_act)
    delta_bf = pull_back(cot_group)[0].astype(jnp.bfloat16)
    local_weight = lax.dot_general(
        aggregate, delta_bf, (((0,), (0,)), ((), ())), preferred_element_type=jnp.float32
    )
    local_bias = jnp.sum(delta_bf.astype(jnp.float32), axis=0)
    feat_rows = local_weight.shape[0]
    packed = jnp.concatenate(
        [local_weight, jnp.broadcast_to(local_bias[None, :], (32, local_bias.shape[0]))], axis=0
    )
    packed = split_sum(packed, "rows", (5, 2), (0, 3, 1, 4))
    grad_weight = packed[:feat_rows]
    grad_bias = packed[feat_rows]
    share_rows = cotangent.shape[0]
    own_act = lax.dynamic_slice_in_dim(activated, replica * share_rows, share_rows, 0)
    return (own_act.astype(jnp.bfloat16), grad_weight, grad_bias)


def solution(mesh):
    in_specs = (
        P("rows", None),
        P("rows"),
        P("rows", "rep", None),
        P("rows", "rep", None),
        P("rows", "rep", None, None),
        P(),
        P(),
        P(("rows", "rep"), None),
    )
    out_specs = (P(("rows", "rep"), None), P(), P())
    return jax.shard_map(layer, mesh=mesh, in_specs=in_specs, out_specs=out_specs, check_vma=False)
```

```python
import jax
import jax.numpy as jnp
from jax import lax
from jax.experimental import pallas as pl
from jax.experimental.pallas import tpu as pltpu
from jax.sharding import PartitionSpec as P


ROWS_BITS = (0, 3, 1, 4, 2, 5)


def from_behind(value, axis, steps):
    count = lax.axis_size(axis)
    pairs = [(source, (source + steps) % count) for source in range(count)]
    return lax.ppermute(value, axis, pairs)


def butterfly_sum(value, axis, order):
    count = lax.axis_size(axis)
    for bit in order:
        if (1 << bit) >= count:
            continue
        pairs = [(source, source ^ (1 << bit)) for source in range(count)]
        value = value + lax.ppermute(value, axis, pairs)
    return value


def gelu_tanh(values):
    return jax.nn.gelu(values, approximate=True)


def _edge_kernel(bufT_ref, far_ref, tgt_ref, out_ref):
    groups, feat, cols = bufT_ref.shape
    blocks, _, slots, edges = far_ref.shape
    col_iota = lax.broadcasted_iota(jnp.int32, (cols, edges), 0)
    row_iota = lax.broadcasted_iota(jnp.int32, (out_ref.shape[1], edges), 0)
    for b in range(blocks):
        acc = jnp.zeros((out_ref.shape[1], feat), jnp.float32)
        for g in range(groups):
            far = far_ref[b, g]
            tgt = tgt_ref[b, g]
            pick = jnp.concatenate(
                [(col_iota == far[k:k + 1, :]).astype(jnp.bfloat16) for k in range(slots)], axis=1
            )
            scatter = jnp.concatenate(
                [(row_iota == tgt[k:k + 1, :]).astype(jnp.bfloat16) for k in range(slots)], axis=1
            )
            pickedT = jnp.dot(bufT_ref[g], pick, preferred_element_type=jnp.float32)
            acc = acc + lax.dot_general(
                scatter, pickedT.astype(jnp.bfloat16), (((1,), (1,)), ((), ())),
                preferred_element_type=jnp.float32,
            )
        out_ref[b] = acc


def edge_sums_kernel(bufT, far, tgt):
    groups, feat, cols = bufT.shape
    blocks = far.shape[0]
    rows = 128
    flops = 2 * blocks * groups * far.shape[2] * (feat * cols * 128 + rows * 128 * feat)
    return pl.pallas_call(
        _edge_kernel,
        out_shape=jax.ShapeDtypeStruct((blocks, rows, feat), jnp.float32),
        in_specs=[pl.BlockSpec(memory_space=pltpu.VMEM)] * 3,
        out_specs=pl.BlockSpec(memory_space=pltpu.VMEM),
        cost_estimate=pl.CostEstimate(
            flops=flops, transcendentals=0,
            bytes_accessed=bufT.size * 2 + far.size * 8 + blocks * rows * feat * 4,
        ),
    )(bufT, far, tgt)


def layer(features, degree, tile_block, edge_count, edge_code, weight, bias, cotangent):
    step_count = tile_block.shape[1]
    replicas = lax.axis_size("rep")
    replica = lax.axis_index("rep")
    inv_deg = lax.rsqrt(degree.astype(jnp.float32))
    scaled = (features.astype(jnp.float32) * inv_deg[:, None]).astype(jnp.bfloat16)

    far = tile_block[..., None] * 128 + edge_code % 128
    is_live = lax.broadcasted_iota(jnp.int32, edge_code.shape, 3) < edge_count[..., None]
    tgt = jnp.where(is_live, edge_code // 128, -1)

    def local_sums(held_t, chosen):
        index = jnp.array(chosen, jnp.int32)
        return edge_sums_kernel(held_t, far[:, index], tgt[:, index])

    row_count = lax.axis_size("rows")
    pairs = []
    for rep_index in range(replicas):
        for source in range(row_count):
            target = (source - step_count * rep_index) % row_count
            pairs.append((source * replicas + rep_index, target * replicas + rep_index))
    held = lax.ppermute(scaled.T, ("rows", "rep"), pairs)[None]
    offsets = [0]
    partial_total = local_sums(held, offsets)
    stride = step_count
    while stride > 1:
        stride //= 2
        arrived = from_behind(held, "rows", -stride)
        arrived_offsets = [offset + stride for offset in offsets]
        partial_total = partial_total + local_sums(arrived, arrived_offsets)
        held = jnp.concatenate([held, arrived], axis=0)
        offsets = offsets + arrived_offsets
    partial_total = partial_total.reshape(-1, partial_total.shape[-1])
    pieces = partial_total.reshape((replicas, -1) + partial_total.shape[1:])
    cot_copies = jnp.broadcast_to(
        cotangent.astype(jnp.float32)[None], (replicas,) + cotangent.shape
    )
    feat_width = pieces.shape[-1]
    pieces = lax.all_to_all(jnp.concatenate([pieces, cot_copies], axis=-1), "rep", 0, 0)
    share = jnp.sum(pieces[..., :feat_width], axis=0)
    cot_group = pieces[..., feat_width:].reshape(-1, cotangent.shape[1])
    copies = jnp.broadcast_to(share[None], (replicas,) + share.shape)
    edge_sums = lax.all_to_all(copies, "rep", 0, 0).reshape(partial_total.shape)
    aggregate = (inv_deg[:, None] * (edge_sums + scaled.astype(jnp.float32))).astype(jnp.bfloat16)
    pre_act = jnp.dot(aggregate, weight, preferred_element_type=jnp.float32) + bias
    activated, pull_back = jax.vjp(gelu_tanh, pre_act)
    delta_bf = pull_back(cot_group)[0].astype(jnp.bfloat16)
    local_weight = lax.dot_general(
        aggregate, delta_bf, (((0,), (0,)), ((), ())), preferred_element_type=jnp.float32
    )
    local_bias = jnp.sum(delta_bf.astype(jnp.float32), axis=0)
    feat_rows = local_weight.shape[0]
    packed = jnp.concatenate(
        [local_weight, jnp.broadcast_to(local_bias[None, :], (8, local_bias.shape[0]))], axis=0
    )
    piece_rows = -(-packed.shape[0] // (8 * replicas)) * 8
    padded = jnp.pad(packed, ((0, piece_rows * replicas - packed.shape[0]), (0, 0)))
    mine = lax.dynamic_index_in_dim(
        padded.reshape((replicas, piece_rows) + packed.shape[1:]), replica, 0, keepdims=False
    )
    mine = butterfly_sum(mine, "rows", ROWS_BITS)
    spread = jnp.broadcast_to(mine[None], (replicas,) + mine.shape)
    packed = lax.all_to_all(spread, "rep", 0, 0).reshape(-1, packed.shape[1])
    grad_weight = packed[:feat_rows]
    grad_bias = packed[feat_rows]
    share_rows = cotangent.shape[0]
    own_act = lax.dynamic_slice_in_dim(activated, replica * share_rows, share_rows, 0)
    return (own_act.astype(jnp.bfloat16), grad_weight, grad_bias)


def solution(mesh):
    in_specs = (
        P("rows", None),
        P("rows"),
        P("rows", "rep", None),
        P("rows", "rep", None),
        P("rows", "rep", None, None),
        P(),
        P(),
        P(("rows", "rep"), None),
    )
    out_specs = (P(("rows", "rep"), None), P(), P())
    return jax.shard_map(layer, mesh=mesh, in_specs=in_specs, out_specs=out_specs, check_vma=False)
```

```python
import jax
import jax.numpy as jnp
from jax import lax
from jax.experimental import pallas as pl
from jax.experimental.pallas import tpu as pltpu
from jax.sharding import PartitionSpec as P


ROWS_BITS = (0, 3, 1, 4, 2, 5)


def from_behind(value, axis, steps):
    count = lax.axis_size(axis)
    pairs = [(source, (source + steps) % count) for source in range(count)]
    return lax.ppermute(value, axis, pairs)


def butterfly_sum(value, axis, order):
    count = lax.axis_size(axis)
    for bit in order:
        if (1 << bit) >= count:
            continue
        pairs = [(source, source ^ (1 << bit)) for source in range(count)]
        value = value + lax.ppermute(value, axis, pairs)
    return value


def gelu_tanh(values):
    return jax.nn.gelu(values, approximate=True)


def _edge_kernel(bufT_ref, far_ref, tgt_ref, out_ref):
    groups, feat, cols = bufT_ref.shape
    blocks, _, slots, edges = far_ref.shape
    col_iota = lax.broadcasted_iota(jnp.int32, (cols, edges), 0)
    row_iota = lax.broadcasted_iota(jnp.int32, (out_ref.shape[1], edges), 0)
    for b in range(blocks):
        acc = jnp.zeros((out_ref.shape[1], feat), jnp.float32)
        for g in range(groups):
            far = far_ref[b, g]
            tgt = tgt_ref[b, g]
            pick = jnp.concatenate(
                [(col_iota == far[k:k + 1, :]).astype(jnp.bfloat16) for k in range(slots)], axis=1
            )
            scatter = jnp.concatenate(
                [(row_iota == tgt[k:k + 1, :]).astype(jnp.bfloat16) for k in range(slots)], axis=1
            )
            pickedT = jnp.dot(bufT_ref[g], pick, preferred_element_type=jnp.float32)
            acc = acc + lax.dot_general(
                scatter, pickedT.astype(jnp.bfloat16), (((1,), (1,)), ((), ())),
                preferred_element_type=jnp.float32,
            )
        out_ref[b] = acc


def edge_sums_kernel(bufT, far, tgt):
    groups, feat, cols = bufT.shape
    blocks = far.shape[0]
    rows = 128
    flops = 2 * blocks * groups * far.shape[2] * (feat * cols * 128 + rows * 128 * feat)
    return pl.pallas_call(
        _edge_kernel,
        out_shape=jax.ShapeDtypeStruct((blocks, rows, feat), jnp.float32),
        in_specs=[pl.BlockSpec(memory_space=pltpu.VMEM)] * 3,
        out_specs=pl.BlockSpec(memory_space=pltpu.VMEM),
        cost_estimate=pl.CostEstimate(
            flops=flops, transcendentals=0,
            bytes_accessed=bufT.size * 2 + far.size * 8 + blocks * rows * feat * 4,
        ),
    )(bufT, far, tgt)


def layer(features, degree, tile_block, edge_count, edge_code, weight, bias, cotangent):
    step_count = tile_block.shape[1]
    replicas = lax.axis_size("rep")
    replica = lax.axis_index("rep")
    inv_deg = lax.rsqrt(degree.astype(jnp.float32))
    scaled = (features.astype(jnp.float32) * inv_deg[:, None]).astype(jnp.bfloat16)

    far = tile_block[..., None] * 128 + edge_code % 128
    is_live = lax.broadcasted_iota(jnp.int32, edge_code.shape, 3) < edge_count[..., None]
    tgt = jnp.where(is_live, edge_code // 128, -1)

    def local_sums(held_t, chosen):
        index = jnp.array(chosen, jnp.int32)
        return edge_sums_kernel(held_t, far[:, index], tgt[:, index])

    row_count = lax.axis_size("rows")
    pairs = []
    for rep_index in range(replicas):
        for source in range(row_count):
            target = (source - step_count * rep_index) % row_count
            pairs.append((source * replicas + rep_index, target * replicas + rep_index))
    held = lax.ppermute(scaled.T, ("rows", "rep"), pairs)[None]
    offsets = [0]
    partial_total = local_sums(held, offsets)
    stride = step_count
    while stride > 1:
        stride //= 2
        arrived = from_behind(held, "rows", -stride)
        arrived_offsets = [offset + stride for offset in offsets]
        partial_total = partial_total + local_sums(arrived, arrived_offsets)
        held = jnp.concatenate([held, arrived], axis=0)
        offsets = offsets + arrived_offsets
    partial_total = partial_total.reshape(-1, partial_total.shape[-1])
    pieces = partial_total.reshape((replicas, -1) + partial_total.shape[1:])
    pieces = lax.all_to_all(pieces.astype(jnp.bfloat16), "rep", 0, 0)
    edge_sums = jnp.sum(pieces.astype(jnp.float32), axis=0)
    share_rows = edge_sums.shape[0]
    share_start = replica * share_rows
    own_rows = lax.dynamic_slice_in_dim(scaled, share_start, share_rows, 0).astype(jnp.float32)
    own_inv = lax.dynamic_slice_in_dim(inv_deg, share_start, share_rows, 0)
    aggregate = (own_inv[:, None] * (edge_sums + own_rows)).astype(jnp.bfloat16)
    pre_act = jnp.dot(aggregate, weight, preferred_element_type=jnp.float32) + bias
    activated, pull_back = jax.vjp(gelu_tanh, pre_act)
    delta_bf = pull_back(cotangent.astype(jnp.float32))[0].astype(jnp.bfloat16)
    local_weight = lax.dot_general(
        aggregate, delta_bf, (((0,), (0,)), ((), ())), preferred_element_type=jnp.float32
    )
    local_bias = jnp.sum(delta_bf.astype(jnp.float32), axis=0)
    feat_rows = local_weight.shape[0]
    packed = jnp.concatenate(
        [local_weight, jnp.broadcast_to(local_bias[None, :], (8, local_bias.shape[0]))], axis=0
    )
    piece_rows = -(-packed.shape[0] // (8 * replicas)) * 8
    padded = jnp.pad(packed, ((0, piece_rows * replicas - packed.shape[0]), (0, 0)))
    parts = lax.all_to_all(
        padded.reshape((replicas, piece_rows) + packed.shape[1:]), "rep", 0, 0
    )
    mine = butterfly_sum(jnp.sum(parts, axis=0), "rows", ROWS_BITS)
    spread = jnp.broadcast_to(mine[None], (replicas,) + mine.shape)
    packed = lax.all_to_all(spread, "rep", 0, 0).reshape(-1, packed.shape[1])
    grad_weight = packed[:feat_rows]
    grad_bias = packed[feat_rows]
    return (activated.astype(jnp.bfloat16), grad_weight, grad_bias)


def solution(mesh):
    in_specs = (
        P("rows", None),
        P("rows"),
        P("rows", "rep", None),
        P("rows", "rep", None),
        P("rows", "rep", None, None),
        P(),
        P(),
        P(("rows", "rep"), None),
    )
    out_specs = (P(("rows", "rep"), None), P(), P())
    return jax.shard_map(layer, mesh=mesh, in_specs=in_specs, out_specs=out_specs, check_vma=False)
```

```python
import jax
import jax.numpy as jnp
from jax import lax
from jax.experimental import pallas as pl
from jax.experimental.pallas import tpu as pltpu
from jax.sharding import PartitionSpec as P


ROWS_BITS = (5, 2, 4, 1, 3, 0)


def from_behind(value, axis, steps):
    count = lax.axis_size(axis)
    pairs = [(source, (source + steps) % count) for source in range(count)]
    return lax.ppermute(value, axis, pairs)


def butterfly_sum(value, axis, order):
    count = lax.axis_size(axis)
    for bit in order:
        if (1 << bit) >= count:
            continue
        pairs = [(source, source ^ (1 << bit)) for source in range(count)]
        value = value + lax.ppermute(value, axis, pairs)
    return value


def gelu_tanh(values):
    return jax.nn.gelu(values, approximate=True)


def _edge_kernel(bufT_ref, far_ref, tgt_ref, out_ref):
    groups, feat, cols = bufT_ref.shape
    blocks, _, slots, edges = far_ref.shape
    col_iota = lax.broadcasted_iota(jnp.int32, (cols, edges), 0)
    row_iota = lax.broadcasted_iota(jnp.int32, (out_ref.shape[1], edges), 0)
    for b in range(blocks):
        acc = jnp.zeros((out_ref.shape[1], feat), jnp.float32)
        for g in range(groups):
            far = far_ref[b, g]
            tgt = tgt_ref[b, g]
            pick = jnp.concatenate(
                [(col_iota == far[k:k + 1, :]).astype(jnp.bfloat16) for k in range(slots)], axis=1
            )
            scatter = jnp.concatenate(
                [(row_iota == tgt[k:k + 1, :]).astype(jnp.bfloat16) for k in range(slots)], axis=1
            )
            pickedT = jnp.dot(bufT_ref[g], pick, preferred_element_type=jnp.float32)
            acc = acc + lax.dot_general(
                scatter, pickedT.astype(jnp.bfloat16), (((1,), (1,)), ((), ())),
                preferred_element_type=jnp.float32,
            )
        out_ref[b] = acc


def edge_sums_kernel(bufT, far, tgt):
    groups, feat, cols = bufT.shape
    blocks = far.shape[0]
    rows = 128
    flops = 2 * blocks * groups * far.shape[2] * (feat * cols * 128 + rows * 128 * feat)
    return pl.pallas_call(
        _edge_kernel,
        out_shape=jax.ShapeDtypeStruct((blocks, rows, feat), jnp.float32),
        in_specs=[pl.BlockSpec(memory_space=pltpu.VMEM)] * 3,
        out_specs=pl.BlockSpec(memory_space=pltpu.VMEM),
        cost_estimate=pl.CostEstimate(
            flops=flops, transcendentals=0,
            bytes_accessed=bufT.size * 2 + far.size * 8 + blocks * rows * feat * 4,
        ),
    )(bufT, far, tgt)


def layer(features, degree, tile_block, edge_count, edge_code, weight, bias, cotangent):
    step_count = tile_block.shape[1]
    replicas = lax.axis_size("rep")
    replica = lax.axis_index("rep")
    inv_deg = lax.rsqrt(degree.astype(jnp.float32))
    scaled = (features.astype(jnp.float32) * inv_deg[:, None]).astype(jnp.bfloat16)

    far = tile_block[..., None] * 128 + edge_code % 128
    is_live = lax.broadcasted_iota(jnp.int32, edge_code.shape, 3) < edge_count[..., None]
    tgt = jnp.where(is_live, edge_code // 128, -1)

    def local_sums(held_t, chosen):
        index = jnp.array(chosen, jnp.int32)
        return edge_sums_kernel(held_t, far[:, index], tgt[:, index])

    row_count = lax.axis_size("rows")
    pairs = []
    for rep_index in range(replicas):
        for source in range(row_count):
            target = (source - step_count * rep_index) % row_count
            pairs.append((source * replicas + rep_index, target * replicas + rep_index))
    held = lax.ppermute(scaled.T, ("rows", "rep"), pairs)[None]
    offsets = [0]
    partial_total = local_sums(held, offsets)
    stride = step_count
    while stride > 1:
        stride //= 2
        arrived = from_behind(held, "rows", -stride)
        arrived_offsets = [offset + stride for offset in offsets]
        partial_total = partial_total + local_sums(arrived, arrived_offsets)
        held = jnp.concatenate([held, arrived], axis=0)
        offsets = offsets + arrived_offsets
    partial_total = partial_total.reshape(-1, partial_total.shape[-1])
    pieces = partial_total.reshape((replicas, -1) + partial_total.shape[1:])
    pieces = lax.all_to_all(pieces, "rep", 0, 0)
    edge_sums = jnp.sum(pieces, axis=0)
    share_rows = edge_sums.shape[0]
    share_start = replica * share_rows
    own_rows = lax.dynamic_slice_in_dim(scaled, share_start, share_rows, 0).astype(jnp.float32)
    own_inv = lax.dynamic_slice_in_dim(inv_deg, share_start, share_rows, 0)
    aggregate = (own_inv[:, None] * (edge_sums + own_rows)).astype(jnp.bfloat16)
    pre_act = jnp.dot(aggregate, weight, preferred_element_type=jnp.float32) + bias
    activated, pull_back = jax.vjp(gelu_tanh, pre_act)
    delta_bf = pull_back(cotangent.astype(jnp.float32))[0].astype(jnp.bfloat16)
    local_weight = lax.dot_general(
        aggregate, delta_bf, (((0,), (0,)), ((), ())), preferred_element_type=jnp.float32
    )
    local_bias = jnp.sum(delta_bf.astype(jnp.float32), axis=0)
    feat_rows = local_weight.shape[0]
    packed = jnp.concatenate(
        [local_weight, jnp.broadcast_to(local_bias[None, :], (8, local_bias.shape[0]))], axis=0
    )
    piece_rows = -(-packed.shape[0] // (8 * replicas)) * 8
    padded = jnp.pad(packed, ((0, piece_rows * replicas - packed.shape[0]), (0, 0)))
    parts = lax.all_to_all(
        padded.reshape((replicas, piece_rows) + packed.shape[1:]), "rep", 0, 0
    )
    mine = butterfly_sum(jnp.sum(parts, axis=0), "rows", ROWS_BITS)
    spread = jnp.broadcast_to(mine[None], (replicas,) + mine.shape)
    packed = lax.all_to_all(spread, "rep", 0, 0).reshape(-1, packed.shape[1])
    grad_weight = packed[:feat_rows]
    grad_bias = packed[feat_rows]
    return (activated.astype(jnp.bfloat16), grad_weight, grad_bias)


def solution(mesh):
    in_specs = (
        P("rows", None),
        P("rows"),
        P("rows", "rep", None),
        P("rows", "rep", None),
        P("rows", "rep", None, None),
        P(),
        P(),
        P(("rows", "rep"), None),
    )
    out_specs = (P(("rows", "rep"), None), P(), P())
    return jax.shard_map(layer, mesh=mesh, in_specs=in_specs, out_specs=out_specs, check_vma=False)
```
